256 devices in a mesh: ctx: 32 (over x, z), head: 8 (over y, core).
Axes of the slice: x: 4, y: 4, z: 8, core: 2. Of those that a mesh axis runs over, the one named last changes fastest.
Arguments:
- queries: bfloat16 [8192, 32, 128], P('ctx', 'head'), may hold values from -40 to 40
- keys: bfloat16 [8192, 8, 128], P('ctx', 'head'), may hold values from -40 to 40
- values: bfloat16 [8192, 8, 128], P('ctx', 'head'), may hold values from -6 to 6
- doc_ids: int32 [8192], P('ctx'), may hold values from 0 to 3, never falling along the last dimension, each value on 1 to 4096 neighbouring positions
Outputs:
- attended: bfloat16 [8192, 4096], P(('ctx', 'head'))
The draws below stay inside these ranges and needn't reach their ends.
Inputs may be any that keep to these rules, and one draw needn't show every extreme that they name: `doc_ids`: document numbers never fall along the sequence; each document has 1 to 4096 tokens and one has exactly 4096.
All inputs are finite; a program needn't handle non-finite values.
Results may differ from the reference program's by a relative error of at most 0.009.
Values may be sent and summed in bfloat16 or wider, within the bound.
No kernel may reach another device: no remote copies, remote signals or barrier semaphores. Data moves between devices by JAX's collectives and lax.ppermute only.
A program may use at most 128 MiB of HBM per device.

```python
import math
import jax
import jax.numpy as jnp
import numpy as np
from jax import lax

QUERY_HEADS = 32
KEY_VALUE_HEADS = 8
HEAD_SIZE = 128
SEGS = 4
SEQUENCE_TOKENS = 8192


def draw_keys(key, part):
    starting_matrix = jax.random.truncated_normal(jax.random.fold_in(key, 2), -6.0, 6.0, (SEQUENCE_TOKENS, KEY_VALUE_HEADS, HEAD_SIZE), jnp.float32)
    return starting_matrix.astype(jnp.bfloat16)


def draw_queries(key, part):
    starting_matrix = jax.random.truncated_normal(jax.random.fold_in(key, 1), -6.0, 6.0, (SEQUENCE_TOKENS, QUERY_HEADS, HEAD_SIZE), jnp.float32)
    return starting_matrix.astype(jnp.bfloat16)


def steps_of(stream_key, extent, split, smallest, high):
    def one(position, shards_of):
        heights = jax.random.uniform(jax.random.fold_in(jax.random.fold_in(stream_key, 6), position), (shards_of,), jnp.float32, smallest / len(split), high / len(split))
        return jnp.repeat(jnp.exp(heights), extent[position] // shards_of).reshape((-1,) + (1,) * (len(extent) - position - 1))

    factor_of = one(*split[0])
    for cut in split[1:]:
        factor_of = factor_of * one(*cut)
    return factor_of


def profile(amount, total, bound, slope):
    loads = [(1 << 20) // math.isqrt(standing ** slope) + 1 for standing in range(2, amount + 1)]
    spare, holding = total - bound - (amount - 1), [1] * (amount - 1)
    while spare > 0:
        candidates = [i for i in range(amount - 1) if holding[i] < bound]
        whole, remaining = sum([loads[i] for i in candidates]), spare
        for i in candidates:
            addition = min(bound - holding[i], max(1, remaining * loads[i] // whole), spare)
            holding[i] = holding[i] + addition
            spare = spare - addition
    return np.array([bound] + holding)


def uneven(stream_key, amount, total, reach, lean):
    if amount == 2:
        one = jax.random.randint(stream_key, (), max(1, total - reach), min(reach, total - 1) + 1)
        return jnp.stack([one, total - one])
    lengths = jnp.asarray(profile(amount, total, reach, lean), jnp.int32)
    twos = (amount - 1) // 2
    giver, taker = lengths[1:1 + 2 * twos:2], lengths[2:2 + 2 * twos:2]
    room = jnp.minimum(giver - 1, reach - taker)
    passed = jax.random.randint(jax.random.fold_in(stream_key, 1), (twos,), 0, 1 << 20) % (room + 1)
    lengths = lengths.at[1:1 + 2 * twos:2].set(giver - passed).at[2:2 + 2 * twos:2].set(taker + passed)
    return lengths[jax.random.permutation(jax.random.fold_in(stream_key, 2), amount)]


def centred(own_key, extent, scale, most, shards=(), kind=jnp.bfloat16):
    entries = jax.random.normal(own_key, extent, jnp.float32) * scale
    if len(shards) > 0:
        entries = steps_of(own_key, extent, shards, -0.22, 0.18) * entries
    return jnp.clip(entries, min=-most, max=most).astype(kind)


def setup_inputs(seed: int = 0) -> dict:
    arg_keys = jax.random.split(jax.random.key(seed), 5)
    return {
        "queries": draw_queries(jax.random.fold_in(arg_keys[4], 71), 0),
        "keys": draw_keys(jax.random.fold_in(arg_keys[4], 71), 0),
        "values": centred(arg_keys[2], (SEQUENCE_TOKENS, KEY_VALUE_HEADS, HEAD_SIZE), 1.0, 6.0, ((0, 32), (1, 8))),
        "doc_ids": jnp.searchsorted(jnp.cumsum(uneven(arg_keys[3], SEGS, SEQUENCE_TOKENS, SEQUENCE_TOKENS // 2, 0)), jnp.arange(SEQUENCE_TOKENS), side="right").astype(jnp.int32),
    }


def reference(queries, keys, values, doc_ids):
    total_len, q_heads, head_dim = queries.shape
    kv_heads = keys.shape[1]
    group_size = q_heads // kv_heads
    block_rows = math.gcd(total_len, 1024)
    block_count = total_len // block_rows
    score_scale = head_dim ** -0.5

    def one_head(head_index):
        kv_index = head_index // group_size
        query_head = lax.dynamic_index_in_dim(queries, head_index, 1, keepdims=False).astype(jnp.float32)
        key_head = lax.dynamic_index_in_dim(keys, kv_index, 1, keepdims=False).astype(jnp.float32)
        value_head = lax.dynamic_index_in_dim(values, kv_index, 1, keepdims=False).astype(jnp.float32)
        key_pos = jnp.arange(total_len, dtype=jnp.int32)

        def one_block(block_index):
            first_row = (block_index * block_rows).astype(jnp.int32)
            query_block = lax.dynamic_slice_in_dim(query_head, first_row, block_rows, 0)
            query_pos = first_row + jnp.arange(block_rows, dtype=jnp.int32)
            query_ids = lax.dynamic_slice_in_dim(doc_ids, first_row, block_rows, 0)
            scores = jnp.dot(query_block, key_head.T, preferred_element_type=jnp.float32,
                             precision=lax.Precision.HIGHEST) * score_scale
            visible = (key_pos[None, :] <= query_pos[:, None]) & (doc_ids[None, :] == query_ids[:, None])
            masked = jnp.where(visible, scores, jnp.float32(-1e30))
            top_score = jnp.max(masked, axis=1, keepdims=True)
            expo = jnp.where(visible, jnp.exp(masked - top_score), jnp.float32(0.0))
            weights = expo / jnp.sum(expo, axis=1, keepdims=True)
            rounded = lax.optimization_barrier(weights.astype(jnp.bfloat16)).astype(jnp.float32)
            return jnp.dot(rounded, value_head, preferred_element_type=jnp.float32,
                           precision=lax.Precision.HIGHEST)

        blocks_out = lax.map(one_block, jnp.arange(block_count, dtype=jnp.int32))
        return blocks_out.reshape(total_len, head_dim)

    heads_out = lax.map(one_head, jnp.arange(q_heads, dtype=jnp.int32))
    joined = jnp.transpose(heads_out, (1, 0, 2)).reshape(total_len, q_heads * head_dim)
    return joined.astype(jnp.bfloat16)
```

```python
import functools
import math

import jax
import jax.numpy as jnp
from jax import lax
from jax.experimental import pallas as pl
from jax.experimental.pallas import tpu as pltpu
from jax.sharding import Mesh
from jax.sharding import PartitionSpec as P


TOK = 256
D = 128
HEADS = 4
NZ = 8
NX = 4
STRIPE = TOK * NZ
HALF = 128
COLS = HALF * HEADS
NEG = -1e30
SHIFTS = (0, 1, -1, 2, -2, 4, 3, -3)


def _scalar(ref, row):
    return jnp.max(ref[row : row + 1, :].astype(jnp.float32)).astype(jnp.int32)


def attn_kernel(deltas, *refs):
    kv = refs[:NZ]
    qs = refs[NZ : NZ + len(deltas)]
    outs = refs[NZ + len(deltas) : NZ + 2 * len(deltas)]
    kscr, vscr, sscr, acc = refs[NZ + 2 * len(deltas) :]
    x, z = lax.axis_index("x"), lax.axis_index("z")
    n1 = n2 = n3 = jnp.int32(0)
    for k, ref in enumerate(kv):
        b = lax.rem(z - SHIFTS[k] + NZ, NZ)
        kscr[b] = ref[0:TOK, :]
        vscr[b, :, 0:HALF] = ref[TOK : TOK + HALF, :]
        vscr[b, :, HALF:TOK] = ref[TOK + HALF : 2 * TOK, :]
        cnt = ref[2 * TOK : 2 * TOK + 8, :].astype(jnp.float32)
        n1 += jnp.max(cnt[1:2, :]).astype(jnp.int32)
        n2 += jnp.max(cnt[2:3, :]).astype(jnp.int32)
        n3 += jnp.max(cnt[3:4, :]).astype(jnp.int32)
    full = jnp.int32(STRIPE)

    for delta, q_ref, o_ref in zip(deltas, qs, outs):
        cnt = q_ref[1024:1032, :].astype(jnp.float32)
        c1 = jnp.max(cnt[1:2, :]).astype(jnp.int32)
        c2 = jnp.max(cnt[2:3, :]).astype(jnp.int32)
        c3 = jnp.max(cnt[3:4, :]).astype(jnp.int32)

        def bounds(tok, delta=delta, c1=c1, c2=c2, c3=c3):
            lo = jnp.where(tok >= c3, n3, jnp.where(tok >= c2, n2, jnp.where(tok >= c1, n1, 0)))
            hi = jnp.where(tok >= c3, full, jnp.where(tok >= c2, n3, jnp.where(tok >= c1, n2, n1)))
            if delta == 0:
                hi = jnp.minimum(hi, z * TOK + tok + 1)
            else:
                hi = jnp.where(x + delta < NX, hi, 0)
            return lo, hi

        def tile(u, _, q_ref=q_ref, o_ref=o_ref, bounds=bounds):
            base = u * HALF
            lo_a, hi_a = bounds(base)
            lo_b, hi_b = bounds(base + HALF - 1)
            k0 = lo_a // TOK
            k1 = jnp.where(hi_b > lo_a, (hi_b + TOK - 1) // TOK, k0)
            ka = jnp.clip((lo_b + TOK - 1) // TOK, k0, k1)
            kb = jnp.clip(hi_a // TOK, ka, k1)
            q = q_ref[pl.ds(pl.multiple_of(u * COLS, COLS), COLS), :]
            tok = (lax.broadcasted_iota(jnp.int32, (1, COLS), 1) & (HALF - 1)) + base
            lo, hi = bounds(tok)

            def scores(masked, c, mx):
                s = lax.dot_general(
                    kscr[c], q, (((1,), (1,)), ((), ())), preferred_element_type=jnp.float32
                )
                if masked:
                    pos = lax.broadcasted_iota(jnp.int32, (TOK, COLS), 0) + c * TOK
                    s = jnp.where((pos >= lo) & (pos < hi), s, NEG)
                sscr[c] = s
                return jnp.maximum(mx, jnp.max(s.reshape(TOK // 8, 8, COLS), axis=0))

            mx = jnp.full((8, COLS), NEG, jnp.float32)
            mx = lax.fori_loop(k0, ka, functools.partial(scores, True), mx)
            mx = lax.fori_loop(ka, kb, functools.partial(scores, False), mx)
            mx = lax.fori_loop(kb, k1, functools.partial(scores, True), mx)
            m = jnp.max(mx, axis=0, keepdims=True)
            acc[...] = jnp.zeros_like(acc)
            scale2 = D**-0.5 * math.log2(math.e)

            def weigh(c, total):
                p = jnp.exp2((sscr[c] - m) * scale2)
                acc[...] += jnp.dot(
                    vscr[c], p.astype(jnp.bfloat16), preferred_element_type=jnp.float32
                )
                return total + jnp.sum(p.reshape(TOK // 8, 8, COLS), axis=0)

            total = lax.fori_loop(k0, k1, weigh, jnp.zeros((8, COLS), jnp.float32))
            total = jnp.maximum(jnp.sum(total, axis=0, keepdims=True), 1e-30)
            lse = m * D**-0.5 + jnp.log(total)
            dt = o_ref.dtype
            h0 = lse.astype(dt)
            r0 = lse - h0.astype(jnp.float32)
            h1 = r0.astype(dt)
            h2 = r0 - h1.astype(jnp.float32)
            row = lax.broadcasted_iota(jnp.int32, (8, COLS), 0)
            stats = jnp.where(
                row == 0,
                h0.astype(jnp.float32),
                jnp.where(row == 1, h1.astype(jnp.float32), jnp.where(row == 2, h2, 0.0)),
            )
            cols = pl.ds(pl.multiple_of(u * COLS, COLS), COLS)
            o_ref[0:D, cols] = (acc[...] * (1.0 / total)).astype(dt)
            o_ref[D : D + 8, cols] = stats.astype(dt)
            return 0

        lax.fori_loop(0, TOK // HALF, tile, 0)


def attn(deltas, kv, qs, dtype):
    n = len(deltas)
    vm = pl.BlockSpec(memory_space=pltpu.VMEM)
    return pl.pallas_call(
        functools.partial(attn_kernel, deltas),
        out_shape=[jax.ShapeDtypeStruct((D + 8, TOK * HEADS), dtype)] * n,
        in_specs=[vm] * (NZ + n),
        out_specs=[vm] * n,
        scratch_shapes=[
            pltpu.VMEM((NZ, TOK, D), jnp.bfloat16),
            pltpu.VMEM((NZ, D, TOK), jnp.bfloat16),
            pltpu.VMEM((NZ, TOK, COLS), jnp.float32),
            pltpu.VMEM((D, COLS), jnp.float32),
        ],
        cost_estimate=pl.CostEstimate(
            flops=4 * 1024 * D * STRIPE * n, bytes_accessed=1 << 20, transcendentals=1024 * STRIPE * n
        ),
    )(*kv, *qs)


def combine_kernel(a_ref, b_ref, c_ref, o_ref):
    x = lax.axis_index("x")

    def lse_of(ref, delta):
        st = ref[D : D + 8, :].astype(jnp.float32)
        lse = st[0:1] + (st[1:2] + st[2:3])
        return jnp.where(x >= delta, lse, NEG) if delta else lse

    la, lb, lc = lse_of(a_ref, 0), lse_of(b_ref, 1), lse_of(c_ref, 2)
    top = jnp.maximum(jnp.maximum(la, lb), lc)
    wa, wb, wc = jnp.exp(la - top), jnp.exp(lb - top), jnp.exp(lc - top)
    inv = 1.0 / (wa + wb + wc)
    wa, wb, wc = wa * inv, wb * inv, wc * inv
    for u in range(TOK // HALF):
        for h in range(HEADS):
            cols = slice((u * HEADS + h) * HALF, (u * HEADS + h + 1) * HALF)
            o = (
                a_ref[0:D, cols].astype(jnp.float32) * wa[:, cols]
                + b_ref[0:D, cols].astype(jnp.float32) * wb[:, cols]
                + c_ref[0:D, cols].astype(jnp.float32) * wc[:, cols]
            )
            o_ref[u * HALF : (u + 1) * HALF, h * D : (h + 1) * D] = o.T.astype(o_ref.dtype)


def combine(a, b, c):
    vm = pl.BlockSpec(memory_space=pltpu.VMEM)
    return pl.pallas_call(
        combine_kernel,
        out_shape=jax.ShapeDtypeStruct((TOK, HEADS * D), jnp.bfloat16),
        in_specs=[vm] * 3,
        out_specs=vm,
    )(a, b, c)


def along(a, axis, shift, n):
    return lax.ppermute(a, axis, [(i, (i + shift) % n) for i in range(n)])


def local(queries, keys, values, doc_ids):
    counts = jnp.sum(
        (doc_ids[None, :] < jnp.arange(8, dtype=jnp.int32)[:, None]).astype(jnp.float32), axis=1
    )
    counts = jnp.broadcast_to(counts[:, None], (8, D)).astype(jnp.bfloat16)
    k = keys.reshape(TOK, D)
    v = jnp.transpose(values.reshape(TOK // HALF, HALF, D), (0, 2, 1)).reshape(TOK, D)
    kv = jnp.concatenate([k, v, counts], axis=0)
    q = jnp.transpose(queries.reshape(TOK // HALF, HALF, HEADS, D), (0, 2, 1, 3)).reshape(-1, D)
    q = jnp.concatenate([q, counts], axis=0)

    up1, dn1 = along(kv, "z", 1, NZ), along(kv, "z", -1, NZ)
    up2, dn2 = along(kv, "z", 2, NZ), along(kv, "z", -2, NZ)
    far = along(kv, "z", 4, NZ)
    up3, dn3 = along(up2, "z", 1, NZ), along(dn2, "z", -1, NZ)
    blocks = [kv, up1, dn1, up2, dn2, far, up3, dn3]
    q1, q2 = along(q, "x", -1, NX), along(q, "x", -2, NX)
    o2, o1 = attn((2, 1), blocks, [q2, q1], jnp.bfloat16)
    r2, r1 = along(o2, "x", 2, NX), along(o1, "x", 1, NX)
    (o0,) = attn((0,), blocks, [q], jnp.float32)
    merged = combine(o0, r1, r2)
    return lax.all_to_all(merged, ("y", "core"), split_axis=0, concat_axis=1, tiled=True)


def solution(mesh):
    grid = Mesh(mesh.devices.reshape(NX, NZ, 4, 2), ("x", "z", "y", "core"))
    ctx, head = ("x", "z"), ("y", "core")
    return jax.shard_map(
        local,
        mesh=grid,
        in_specs=(P(ctx, head, None), P(ctx, head, None), P(ctx, head, None), P(ctx)),
        out_specs=P(ctx + head, None),
        check_vma=False,
    )
```

```python
import functools
import math

import jax
import jax.numpy as jnp
from jax import lax
from jax.experimental import pallas as pl
from jax.experimental.pallas import tpu as pltpu
from jax.sharding import Mesh
from jax.sharding import PartitionSpec as P


TOK = 256
D = 128
HEADS = 4
NZ = 8
NX = 4
STRIPE = TOK * NZ
HALF = 128
COLS = HALF * HEADS
NEG = -1e30
SHIFTS = (0, 1, -1, 2, -2, 4, 3, -3)
NEAR = 5
MIB = 1 << 20


def prep_kernel(k_ref, v_ref, ids_ref, kv_ref, cnt_ref):
    kv_ref[0:TOK, :] = k_ref[...]
    for i in range(TOK // HALF):
        kv_ref[TOK + i * HALF : TOK + (i + 1) * HALF, :] = v_ref[i * HALF : (i + 1) * HALF, :].T
    ids = ids_ref[...]
    row = lax.broadcasted_iota(jnp.int32, (8, D), 0)
    cnt = jnp.zeros((8, D), jnp.float32)
    for d in (1, 2, 3):
        n = jnp.sum(jnp.where(ids < d, 1.0, 0.0))
        cnt = jnp.where(row == d, n, cnt)
    cnt = cnt.astype(jnp.bfloat16)
    kv_ref[2 * TOK : 2 * TOK + 8, :] = cnt
    cnt_ref[...] = cnt


def prep(k, v, ids):
    vm = pl.BlockSpec(memory_space=pltpu.VMEM)
    return pl.pallas_call(
        prep_kernel,
        out_shape=[
            jax.ShapeDtypeStruct((2 * TOK + 8, D), jnp.bfloat16),
            jax.ShapeDtypeStruct((8, D), jnp.bfloat16),
        ],
        in_specs=[vm] * 3,
        out_specs=[vm] * 2,
        compiler_params=pltpu.CompilerParams(vmem_limit_bytes=4 * MIB),
    )(k, v, ids)


def attn_kernel(deltas, shifts, merge, *refs):
    n, nb = len(deltas), len(shifts)
    kv, refs = refs[:nb], refs[nb:]
    qs, refs = refs[:n], refs[n:]
    before, refs = (refs[:n], refs[n:]) if merge else (None, refs)
    outs, (kscr, vscr, sscr, acc, cscr) = refs[:n], refs[n:]
    x, z = lax.axis_index("x"), lax.axis_index("z")
    for i, ref in enumerate(kv):
        kscr[i] = ref[0:TOK, :]
        vscr[i, :, 0:HALF] = ref[TOK : TOK + HALF, :]
        vscr[i, :, HALF:TOK] = ref[TOK + HALF : 2 * TOK, :]
        cnt = ref[2 * TOK : 2 * TOK + 8, :].astype(jnp.float32)
        cscr[i, 0] = lax.rem(z - shifts[i] + NZ, NZ)
        for d in (1, 2, 3):
            cscr[i, d] = jnp.max(cnt[d : d + 1, :]).astype(jnp.int32)

    for j, delta in enumerate(deltas):
        q_ref, o_ref = qs[j], outs[j]
        cnt = q_ref[1024:1032, :].astype(jnp.float32)
        ends = [jnp.max(cnt[d : d + 1, :]).astype(jnp.int32) for d in (1, 2, 3)]

        def pick(tok, a, b, c, d, ends=ends):
            return jnp.where(
                tok >= ends[2], d, jnp.where(tok >= ends[1], c, jnp.where(tok >= ends[0], b, a))
            )

        def bounds(i, tok, delta=delta, pick=pick):
            c1, c2, c3 = cscr[i, 1], cscr[i, 2], cscr[i, 3]
            lo = pick(tok, jnp.int32(0), c1, c2, c3)
            hi = pick(tok, c1, c2, c3, jnp.int32(TOK))
            if delta == 0:
                b = cscr[i, 0]
                hi = jnp.minimum(hi, jnp.where(b < z, TOK, jnp.where(b == z, tok + 1, 0)))
            else:
                hi = jnp.where(x + delta < NX, hi, 0)
            return lo, hi

        def tile(u, _, j=j, q_ref=q_ref, o_ref=o_ref, bounds=bounds):
            base = u * HALF
            cols = pl.ds(pl.multiple_of(u * COLS, COLS), COLS)
            q = q_ref[cols, :]
            tok = (lax.broadcasted_iota(jnp.int32, (1, COLS), 1) & (HALF - 1)) + base

            def state(i):
                lo_a, hi_a = bounds(i, base)
                lo_b, hi_b = bounds(i, base + HALF - 1)
                seen = hi_b > lo_a
                whole = (lo_b <= 0) & (hi_a >= TOK)
                return jnp.where(seen, jnp.where(whole, 2, 1), 0)

            def scores(masked, i, mx):
                s = lax.dot_general(
                    kscr[i], q, (((1,), (1,)), ((), ())), preferred_element_type=jnp.float32
                )
                if masked:
                    lo, hi = bounds(i, tok)
                    pos = lax.broadcasted_iota(jnp.int32, (TOK, COLS), 0)
                    s = jnp.where((pos >= lo) & (pos < hi), s, NEG)
                sscr[i] = s
                return jnp.maximum(mx, jnp.max(s.reshape(TOK // 8, 8, COLS), axis=0))

            def first_pass(i, mx):
                return lax.switch(
                    state(i),
                    (
                        lambda mx: mx,
                        functools.partial(scores, True, i),
                        functools.partial(scores, False, i),
                    ),
                    mx,
                )

            mx = lax.fori_loop(0, nb, first_pass, jnp.full((8, COLS), NEG, jnp.float32))
            m = jnp.max(mx, axis=0, keepdims=True)
            acc[...] = jnp.zeros_like(acc)
            scale2 = D**-0.5 * math.log2(math.e)

            def weigh(i, total):
                p = jnp.exp2((sscr[i] - m) * scale2)
                acc[...] += jnp.dot(
                    vscr[i], p.astype(jnp.bfloat16), preferred_element_type=jnp.float32
                )
                return total + jnp.sum(p.reshape(TOK // 8, 8, COLS), axis=0)

            def second_pass(i, total):
                return lax.cond(state(i) > 0, functools.partial(weigh, i), lambda t: t, total)

            total = lax.fori_loop(0, nb, second_pass, jnp.zeros((8, COLS), jnp.float32))
            total = jnp.maximum(jnp.sum(total, axis=0, keepdims=True), 1e-30)
            lse = m * D**-0.5 + jnp.log(total)
            inv = 1.0 / total
            if merge:
                old = before[j][D : D + 1, cols]
                top = jnp.maximum(lse, old)
                w, w_old = jnp.exp(lse - top), jnp.exp(old - top)
                lse = top + jnp.log(w + w_old)
                share = 1.0 / (w + w_old)
                out = acc[...] * (w * share * inv) + before[j][0:D, cols] * (w_old * share)
            else:
                out = acc[...] * inv
            dt = o_ref.dtype
            h0 = lse.astype(dt)
            r0 = lse - h0.astype(jnp.float32)
            h1 = r0.astype(dt)
            h2 = r0 - h1.astype(jnp.float32)
            row = lax.broadcasted_iota(jnp.int32, (8, COLS), 0)
            stats = jnp.where(
                row == 0,
                h0.astype(jnp.float32),
                jnp.where(row == 1, h1.astype(jnp.float32), jnp.where(row == 2, h2, 0.0)),
            )
            o_ref[0:D, cols] = out.astype(dt)
            o_ref[D : D + 8, cols] = stats.astype(dt)
            return 0

        lax.fori_loop(0, TOK // HALF, tile, 0)


def attn(deltas, shifts, kv, qs, before, dtype):
    n, nb = len(deltas), len(shifts)
    vm = pl.BlockSpec(memory_space=pltpu.VMEM)
    args = (*kv, *qs, *before)
    return pl.pallas_call(
        functools.partial(attn_kernel, deltas, shifts, bool(before)),
        out_shape=[jax.ShapeDtypeStruct((D + 8, TOK * HEADS), dtype)] * n,
        in_specs=[vm] * len(args),
        out_specs=[vm] * n,
        scratch_shapes=[
            pltpu.VMEM((nb, TOK, D), jnp.bfloat16),
            pltpu.VMEM((nb, D, TOK), jnp.bfloat16),
            pltpu.VMEM((nb, TOK, COLS), jnp.float32),
            pltpu.VMEM((D, COLS), jnp.float32),
            pltpu.SMEM((nb, 4), jnp.int32),
        ],
        compiler_params=pltpu.CompilerParams(vmem_limit_bytes=12 * MIB),
        cost_estimate=pl.CostEstimate(
            flops=4 * 1024 * D * TOK * nb * n,
            bytes_accessed=MIB,
            transcendentals=1024 * TOK * nb * n,
        ),
    )(*args)


def combine_kernel(a_ref, b_ref, c_ref, o_ref):
    x = lax.axis_index("x")

    def lse_of(ref, delta):
        st = ref[D : D + 8, :].astype(jnp.float32)
        lse = st[0:1] + (st[1:2] + st[2:3])
        return jnp.where(x >= delta, lse, NEG) if delta else lse

    la, lb, lc = lse_of(a_ref, 0), lse_of(b_ref, 1), lse_of(c_ref, 2)
    top = jnp.maximum(jnp.maximum(la, lb), lc)
    wa, wb, wc = jnp.exp(la - top), jnp.exp(lb - top), jnp.exp(lc - top)
    inv = 1.0 / (wa + wb + wc)
    wa, wb, wc = wa * inv, wb * inv, wc * inv
    for u in range(TOK // HALF):
        for h in range(HEADS):
            cols = slice((u * HEADS + h) * HALF, (u * HEADS + h + 1) * HALF)
            o = (
                a_ref[0:D, cols].astype(jnp.float32) * wa[:, cols]
                + b_ref[0:D, cols].astype(jnp.float32) * wb[:, cols]
                + c_ref[0:D, cols].astype(jnp.float32) * wc[:, cols]
            )
            o_ref[u * HALF : (u + 1) * HALF, h * D : (h + 1) * D] = o.T.astype(o_ref.dtype)


def combine(a, b, c):
    vm = pl.BlockSpec(memory_space=pltpu.VMEM)
    return pl.pallas_call(
        combine_kernel,
        out_shape=jax.ShapeDtypeStruct((TOK, HEADS * D), jnp.bfloat16),
        in_specs=[vm] * 3,
        out_specs=vm,
        compiler_params=pltpu.CompilerParams(vmem_limit_bytes=6 * MIB),
    )(a, b, c)


def along(a, axis, shift, n):
    return lax.ppermute(a, axis, [(i, (i + shift) % n) for i in range(n)])


def local(queries, keys, values, doc_ids):
    kv, counts = prep(keys.reshape(TOK, D), values.reshape(TOK, D), doc_ids.reshape(2, D))
    q = jnp.transpose(queries.reshape(TOK // HALF, HALF, HEADS, D), (0, 2, 1, 3)).reshape(-1, D)
    q = jnp.concatenate([q, counts], axis=0)

    up1, dn1 = along(kv, "z", 1, NZ), along(kv, "z", -1, NZ)
    up2, dn2 = along(kv, "z", 2, NZ), along(kv, "z", -2, NZ)
    far = along(kv, "z", 4, NZ)
    up3, dn3 = along(up2, "z", 1, NZ), along(dn2, "z", -1, NZ)
    blocks = [kv, up1, dn1, up2, dn2, far, up3, dn3]
    q1, q2 = along(q, "x", -1, NX), along(q, "x", -2, NX)
    near = attn((2, 1), SHIFTS[:NEAR], blocks[:NEAR], [q2, q1], (), jnp.float32)
    o2, o1 = attn((2, 1), SHIFTS[NEAR:], blocks[NEAR:], [q2, q1], near, jnp.bfloat16)
    r2, r1 = along(o2, "x", 2, NX), along(o1, "x", 1, NX)
    (o0,) = attn((0,), SHIFTS, blocks, [q], (), jnp.float32)
    merged = combine(o0, r1, r2)
    return lax.all_to_all(merged, ("y", "core"), split_axis=0, concat_axis=1, tiled=True)


def solution(mesh):
    grid = Mesh(mesh.devices.reshape(NX, NZ, 4, 2), ("x", "z", "y", "core"))
    ctx, head = ("x", "z"), ("y", "core")
    return jax.shard_map(
        local,
        mesh=grid,
        in_specs=(P(ctx, head, None), P(ctx, head, None), P(ctx, head, None), P(ctx)),
        out_specs=P(ctx + head, None),
        check_vma=False,
    )
```

```python
import functools
import math

import jax
import jax.numpy as jnp
from jax import lax
from jax.experimental import pallas as pl
from jax.experimental.pallas import tpu as pltpu
from jax.sharding import Mesh
from jax.sharding import PartitionSpec as P


TOK = 256
D = 128
HEADS = 4
NZ = 8
NX = 4
STRIPE = TOK * NZ
HALF = 128
COLS = HALF * HEADS
NEG = -1e30
SHIFTS = (0, 1, -1, 2, -2, 4, 3, -3)
NEAR = 5
MIB = 1 << 20
ROWS = TOK * HEADS
GROUPS = ROWS // HALF
SCALE = D**-0.5
SCALE2 = SCALE * math.log2(math.e)
VM = pl.BlockSpec(memory_space=pltpu.VMEM)


def prep_kernel(k_ref, v_ref, ids_ref, kv_ref, cnt_ref):
    kv_ref[0:TOK, :] = k_ref[...]
    kv_ref[TOK : 2 * TOK, :] = v_ref[...]
    ids = ids_ref[...]
    row = lax.broadcasted_iota(jnp.int32, (8, D), 0)
    cnt = jnp.zeros((8, D), jnp.float32)
    for d in (1, 2, 3):
        n = jnp.sum(jnp.where(ids < d, 1.0, 0.0))
        cnt = jnp.where(row == d, n, cnt)
    cnt = cnt.astype(jnp.bfloat16)
    kv_ref[2 * TOK : 2 * TOK + 8, :] = cnt
    cnt_ref[...] = cnt


def prep(k, v, ids):
    return pl.pallas_call(
        prep_kernel,
        out_shape=[
            jax.ShapeDtypeStruct((2 * TOK + 8, D), jnp.bfloat16),
            jax.ShapeDtypeStruct((8, D), jnp.bfloat16),
        ],
        in_specs=[VM] * 3,
        out_specs=[VM] * 2,
        compiler_params=pltpu.CompilerParams(vmem_limit_bytes=4 * MIB),
    )(k, v, ids)


def attn_kernel(deltas, shifts, merge, last, *refs):
    n, nb = len(deltas), len(shifts)
    kv, refs = refs[:nb], refs[nb:]
    qs, refs = refs[:n], refs[n:]
    before, refs = (refs[: 3 * n], refs[3 * n :]) if merge else (None, refs)
    per = {"state": 3, "send": 1, "keep": 2}[last]
    outs, (kscr, vscr, sscr, acc, mscr, lscr, rows_scr, cscr) = refs[: per * n], refs[per * n :]
    x, z = lax.axis_index("x"), lax.axis_index("z")
    for i, ref in enumerate(kv):
        kscr[i] = ref[0:TOK, :]
        vscr[i] = ref[TOK : 2 * TOK, :]
        cnt = ref[2 * TOK : 2 * TOK + 8, :].astype(jnp.float32)
        cscr[i, 0] = lax.rem(z - shifts[i] + NZ, NZ)
        for d in (1, 2, 3):
            cscr[i, d] = jnp.max(cnt[d : d + 1, :]).astype(jnp.int32)

    for j, delta in enumerate(deltas):
        q_ref = qs[j]
        cnt = q_ref[ROWS : ROWS + 8, :].astype(jnp.float32)
        ends = [jnp.max(cnt[d : d + 1, :]).astype(jnp.int32) for d in (1, 2, 3)]

        def pick(tok, a, b, c, d, ends=ends):
            return jnp.where(
                tok >= ends[2], d, jnp.where(tok >= ends[1], c, jnp.where(tok >= ends[0], b, a))
            )

        def bounds(i, tok, delta=delta, pick=pick):
            c1, c2, c3 = cscr[i, 1], cscr[i, 2], cscr[i, 3]
            lo = pick(tok, jnp.int32(0), c1, c2, c3)
            hi = pick(tok, c1, c2, c3, jnp.int32(TOK))
            if delta == 0:
                b = cscr[i, 0]
                hi = jnp.minimum(hi, jnp.where(b < z, TOK, jnp.where(b == z, tok + 1, 0)))
            else:
                hi = jnp.where(x + delta < NX, hi, 0)
            return lo, hi

        def tile(u, _, j=j, q_ref=q_ref, bounds=bounds):
            base = u * HALF
            rows = pl.ds(pl.multiple_of(u * COLS, COLS), COLS)

            def state(i):
                lo_a, hi_a = bounds(i, base)
                lo_b, hi_b = bounds(i, base + HALF - 1)
                seen = hi_b > lo_a
                whole = (lo_b <= 0) & (hi_a >= TOK)
                return jnp.where(seen, jnp.where(whole, 2, 1), 0)

            def scores(masked, i):
                s = lax.dot_general(
                    q_ref[rows, :],
                    kscr[i],
                    (((1,), (1,)), ((), ())),
                    preferred_element_type=jnp.float32,
                )
                if masked:
                    tok = lax.broadcasted_iota(jnp.int32, (HALF, TOK), 0) + base
                    pos = lax.broadcasted_iota(jnp.int32, (HALF, TOK), 1)
                    lo, hi = bounds(i, tok)
                    seen = (pos >= lo) & (pos < hi)
                    s = jnp.concatenate(
                        [jnp.where(seen, s[h * HALF : (h + 1) * HALF], NEG) for h in range(HEADS)],
                        axis=0,
                    )
                sscr[i] = s
                mscr[...] = jnp.maximum(mscr[...], jnp.maximum(s[:, 0:D], s[:, D : 2 * D]))

            def first_pass(i, _):
                st = state(i)
                pl.when(st == 1)(lambda: scores(True, i))
                pl.when(st == 2)(lambda: scores(False, i))
                return 0

            mscr[...] = before[3 * j + 1][rows, :] if merge else jnp.full((COLS, D), NEG, jnp.float32)
            lax.fori_loop(0, nb, first_pass, 0)
            m = jnp.max(mscr[...], axis=1, keepdims=True)
            if merge:
                shrink = jnp.exp2((before[3 * j + 1][rows, :] - m) * SCALE2)
                acc[...] = before[3 * j][rows, :] * shrink
                lscr[...] = before[3 * j + 2][rows, :] * shrink
            else:
                acc[...] = jnp.zeros_like(acc)
                lscr[...] = jnp.zeros_like(lscr)

            def weigh(i):
                p = jnp.exp2((sscr[i] - m) * SCALE2)
                lscr[...] += p[:, 0:D] + p[:, D : 2 * D]
                acc[...] += jnp.dot(
                    p.astype(jnp.bfloat16), vscr[i], preferred_element_type=jnp.float32
                )

            def second_pass(i, _):
                pl.when(state(i) > 0)(lambda: weigh(i))
                return 0

            lax.fori_loop(0, nb, second_pass, 0)
            if last == "state":
                outs[3 * j][rows, :] = acc[...]
                outs[3 * j + 1][rows, :] = jnp.broadcast_to(m, (COLS, D))
                outs[3 * j + 2][rows, :] = lscr[...]
                return 0
            total = jnp.maximum(jnp.sum(lscr[...], axis=1, keepdims=True), 1e-30)
            outs[per * j][rows, :] = (acc[...] * (1.0 / total)).astype(outs[per * j].dtype)
            lse = jnp.broadcast_to(m * SCALE + jnp.log(total), (COLS, D))
            for h in range(HEADS):
                rows_scr[pl.ds(u * HEADS + h, 1), :] = lse[h * HALF : (h + 1) * HALF, :].T[0:1, :]
            return 0

        lax.fori_loop(0, TOK // HALF, tile, 0)
        if last == "keep":
            outs[2 * j + 1][...] = rows_scr[...]
        elif last == "send":
            rest = rows_scr[...]
            for t in range(3):
                part = rest.astype(jnp.bfloat16)
                outs[j][ROWS + t * GROUPS : ROWS + (t + 1) * GROUPS, :] = part
                rest = rest - part.astype(jnp.float32)


def attn(deltas, shifts, kv, qs, before, last):
    n, nb = len(deltas), len(shifts)
    args = (*kv, *qs, *before)
    wide = jax.ShapeDtypeStruct((ROWS, D), jnp.float32)
    outs = {
        "state": [wide] * 3,
        "send": [jax.ShapeDtypeStruct((ROWS + 3 * GROUPS, D), jnp.bfloat16)],
        "keep": [wide, jax.ShapeDtypeStruct((GROUPS, D), jnp.float32)],
    }[last] * n
    return pl.pallas_call(
        functools.partial(attn_kernel, deltas, shifts, bool(before), last),
        out_shape=outs,
        in_specs=[VM] * len(args),
        out_specs=[VM] * len(outs),
        scratch_shapes=[
            pltpu.VMEM((nb, TOK, D), jnp.bfloat16),
            pltpu.VMEM((nb, TOK, D), jnp.bfloat16),
            pltpu.VMEM((nb, COLS, TOK), jnp.float32),
            pltpu.VMEM((COLS, D), jnp.float32),
            pltpu.VMEM((COLS, D), jnp.float32),
            pltpu.VMEM((COLS, D), jnp.float32),
            pltpu.VMEM((GROUPS, D), jnp.float32),
            pltpu.SMEM((nb, 4), jnp.int32),
        ],
        compiler_params=pltpu.CompilerParams(vmem_limit_bytes=12 * MIB),
        cost_estimate=pl.CostEstimate(
            flops=4 * ROWS * D * TOK * nb * n,
            bytes_accessed=MIB,
            transcendentals=ROWS * TOK * nb * n,
        ),
    )(*args)


def combine_kernel(a_ref, lse_ref, b_ref, c_ref, o_ref):
    x = lax.axis_index("x")

    def lse_of(ref, delta):
        terms = [
            ref[ROWS + t * GROUPS : ROWS + (t + 1) * GROUPS, :].astype(jnp.float32)
            for t in range(3)
        ]
        return jnp.where(x >= delta, terms[0] + (terms[1] + terms[2]), NEG)

    lses = (lse_ref[...], lse_of(b_ref, 1), lse_of(c_ref, 2))
    top = jnp.maximum(jnp.maximum(lses[0], lses[1]), lses[2])
    ws = [jnp.exp(lse - top) for lse in lses]
    inv = 1.0 / (ws[0] + ws[1] + ws[2])
    pad = jnp.zeros((HALF - GROUPS, D), jnp.float32)
    ws = [jnp.concatenate([w * inv, pad], axis=0).T for w in ws]
    for g in range(GROUPS):
        u, h = divmod(g, HEADS)
        rows = slice(g * HALF, (g + 1) * HALF)
        o = sum(
            ref[rows, :].astype(jnp.float32) * w[:, g : g + 1]
            for ref, w in zip((a_ref, b_ref, c_ref), ws)
        )
        o_ref[u * HALF : (u + 1) * HALF, h * D : (h + 1) * D] = o.astype(o_ref.dtype)


def combine(*args):
    return pl.pallas_call(
        combine_kernel,
        out_shape=jax.ShapeDtypeStruct((TOK, HEADS * D), jnp.bfloat16),
        in_specs=[VM] * len(args),
        out_specs=VM,
        compiler_params=pltpu.CompilerParams(vmem_limit_bytes=6 * MIB),
    )(*args)


def along(a, axis, shift, n):
    return lax.ppermute(a, axis, [(i, (i + shift) % n) for i in range(n)])


def local(queries, keys, values, doc_ids):
    kv, counts = prep(keys.reshape(TOK, D), values.reshape(TOK, D), doc_ids.reshape(2, D))
    q = jnp.transpose(queries.reshape(TOK // HALF, HALF, HEADS, D), (0, 2, 1, 3)).reshape(-1, D)
    q = jnp.concatenate([q, counts], axis=0)

    up1, dn1 = along(kv, "z", 1, NZ), along(kv, "z", -1, NZ)
    up2, dn2 = along(kv, "z", 2, NZ), along(kv, "z", -2, NZ)
    far = along(kv, "z", 4, NZ)
    up3, dn3 = along(up2, "z", 1, NZ), along(dn2, "z", -1, NZ)
    blocks = [kv, up1, dn1, up2, dn2, far, up3, dn3]
    q1, q2 = along(q, "x", -1, NX), along(q, "x", -2, NX)
    near = attn((2, 1), SHIFTS[:NEAR], blocks[:NEAR], [q2, q1], (), "state")
    (o2,) = attn((2,), SHIFTS[NEAR:], blocks[NEAR:], [q2], near[:3], "send")
    r2 = along(o2, "x", 2, NX)
    (o1,) = attn((1,), SHIFTS[NEAR:], blocks[NEAR:], [q1], near[3:], "send")
    r1 = along(o1, "x", 1, NX)
    o0, lse0 = attn((0,), SHIFTS, blocks, [q], (), "keep")
    merged = combine(o0, lse0, r1, r2)
    return lax.all_to_all(merged, ("y", "core"), split_axis=0, concat_axis=1, tiled=True)


def solution(mesh):
    grid = Mesh(mesh.devices.reshape(NX, NZ, 4, 2), ("x", "z", "y", "core"))
    ctx, head = ("x", "z"), ("y", "core")
    return jax.shard_map(
        local,
        mesh=grid,
        in_specs=(P(ctx, head, None), P(ctx, head, None), P(ctx, head, None), P(ctx)),
        out_specs=P(ctx + head, None),
        check_vma=False,
    )
```

```python
import functools
import math

import jax
import jax.numpy as jnp
from jax import lax
from jax.experimental import pallas as pl
from jax.experimental.pallas import tpu as pltpu
from jax.sharding import Mesh
from jax.sharding import PartitionSpec as P


TOK = 256
D = 128
HEADS = 4
NZ = 8
NX = 4
STRIPE = TOK * NZ
HALF = 128
COLS = HALF * HEADS
NEG = -1e30
SHIFTS = (0, -1, -2, 1, 2, 4, 3, -3)
NEAR = 3
MIB = 1 << 20
ROWS = TOK * HEADS
GROUPS = ROWS // HALF
SCALE = D**-0.5
SCALE2 = SCALE * math.log2(math.e)
VM = pl.BlockSpec(memory_space=pltpu.VMEM)


def prep_kernel(k_ref, v_ref, ids_ref, kv_ref, cnt_ref):
    kv_ref[0:TOK, :] = k_ref[...]
    kv_ref[TOK : 2 * TOK, :] = v_ref[...]
    ids = ids_ref[...]
    row = lax.broadcasted_iota(jnp.int32, (8, D), 0)
    cnt = jnp.zeros((8, D), jnp.float32)
    for d in (1, 2, 3):
        n = jnp.sum(jnp.where(ids < d, 1.0, 0.0))
        cnt = jnp.where(row == d, n, cnt)
    cnt = cnt.astype(jnp.bfloat16)
    kv_ref[2 * TOK : 2 * TOK + 8, :] = cnt
    cnt_ref[...] = cnt


def prep(k, v, ids):
    return pl.pallas_call(
        prep_kernel,
        out_shape=[
            jax.ShapeDtypeStruct((2 * TOK + 8, D), jnp.bfloat16),
            jax.ShapeDtypeStruct((8, D), jnp.bfloat16),
        ],
        in_specs=[VM] * 3,
        out_specs=[VM] * 2,
        compiler_params=pltpu.CompilerParams(vmem_limit_bytes=4 * MIB),
    )(k, v, ids)


def attn_kernel(deltas, shifts, merge, last, *refs):
    n, nb = len(deltas), len(shifts)
    kv, refs = refs[:nb], refs[nb:]
    qs, refs = refs[:n], refs[n:]
    before, refs = (refs[: 3 * n], refs[3 * n :]) if merge else (None, refs)
    per = {"state": 3, "send": 1, "keep": 2}[last]
    outs, (kscr, vscr, sscr, acc, mscr, lscr, rows_scr, cscr) = refs[: per * n], refs[per * n :]
    x, z = lax.axis_index("x"), lax.axis_index("z")
    for i, ref in enumerate(kv):
        kscr[i] = ref[0:TOK, :]
        vscr[i] = ref[TOK : 2 * TOK, :]
        cnt = ref[2 * TOK : 2 * TOK + 8, :].astype(jnp.float32)
        cscr[i, 0] = lax.rem(z - shifts[i] + NZ, NZ)
        for d in (1, 2, 3):
            cscr[i, d] = jnp.max(cnt[d : d + 1, :]).astype(jnp.int32)

    for j, delta in enumerate(deltas):
        q_ref = qs[j]
        cnt = q_ref[ROWS : ROWS + 8, :].astype(jnp.float32)
        ends = [jnp.max(cnt[d : d + 1, :]).astype(jnp.int32) for d in (1, 2, 3)]

        def pick(tok, a, b, c, d, ends=ends):
            return jnp.where(
                tok >= ends[2], d, jnp.where(tok >= ends[1], c, jnp.where(tok >= ends[0], b, a))
            )

        def bounds(i, tok, delta=delta, pick=pick):
            c1, c2, c3 = cscr[i, 1], cscr[i, 2], cscr[i, 3]
            lo = pick(tok, jnp.int32(0), c1, c2, c3)
            hi = pick(tok, c1, c2, c3, jnp.int32(TOK))
            if delta == 0:
                b = cscr[i, 0]
                hi = jnp.minimum(hi, jnp.where(b < z, TOK, jnp.where(b == z, tok + 1, 0)))
            else:
                hi = jnp.where(x + delta < NX, hi, 0)
            return lo, hi

        def tile(u, _, j=j, q_ref=q_ref, bounds=bounds):
            base = u * HALF
            rows = pl.ds(pl.multiple_of(u * COLS, COLS), COLS)

            def state(i):
                lo_a, hi_a = bounds(i, base)
                lo_b, hi_b = bounds(i, base + HALF - 1)
                seen = hi_b > lo_a
                whole = (lo_b <= 0) & (hi_a >= TOK)
                return jnp.where(seen, jnp.where(whole, 2, 1), 0)

            def scores(masked, i):
                s = lax.dot_general(
                    q_ref[rows, :],
                    kscr[i],
                    (((1,), (1,)), ((), ())),
                    preferred_element_type=jnp.float32,
                )
                if masked:
                    tok = lax.broadcasted_iota(jnp.int32, (HALF, TOK), 0) + base
                    pos = lax.broadcasted_iota(jnp.int32, (HALF, TOK), 1)
                    lo, hi = bounds(i, tok)
                    seen = (pos >= lo) & (pos < hi)
                    s = jnp.concatenate(
                        [jnp.where(seen, s[h * HALF : (h + 1) * HALF], NEG) for h in range(HEADS)],
                        axis=0,
                    )
                sscr[i] = s
                mscr[...] = jnp.maximum(mscr[...], jnp.maximum(s[:, 0:D], s[:, D : 2 * D]))

            def first_pass(i, _):
                st = state(i)
                pl.when(st == 1)(lambda: scores(True, i))
                pl.when(st == 2)(lambda: scores(False, i))
                return 0

            mscr[...] = before[3 * j + 1][rows, :] if merge else jnp.full((COLS, D), NEG, jnp.float32)
            lax.fori_loop(0, nb, first_pass, 0)
            m = jnp.max(mscr[...], axis=1, keepdims=True)
            if merge:
                shrink = jnp.exp2((before[3 * j + 1][rows, :] - m) * SCALE2)
                acc[...] = before[3 * j][rows, :] * shrink
                lscr[...] = before[3 * j + 2][rows, :] * shrink
            else:
                acc[...] = jnp.zeros_like(acc)
                lscr[...] = jnp.zeros_like(lscr)

            def weigh(i):
                p = jnp.exp2((sscr[i] - m) * SCALE2)
                lscr[...] += p[:, 0:D] + p[:, D : 2 * D]
                acc[...] += jnp.dot(
                    p.astype(jnp.bfloat16), vscr[i], preferred_element_type=jnp.float32
                )

            def second_pass(i, _):
                pl.when(state(i) > 0)(lambda: weigh(i))
                return 0

            lax.fori_loop(0, nb, second_pass, 0)
            if last == "state":
                outs[3 * j][rows, :] = acc[...]
                outs[3 * j + 1][rows, :] = jnp.broadcast_to(m, (COLS, D))
                outs[3 * j + 2][rows, :] = lscr[...]
                return 0
            total = jnp.maximum(jnp.sum(lscr[...], axis=1, keepdims=True), 1e-30)
            outs[per * j][rows, :] = (acc[...] * (1.0 / total)).astype(outs[per * j].dtype)
            lse = jnp.broadcast_to(m * SCALE + jnp.log(total), (COLS, D))
            for h in range(HEADS):
                rows_scr[pl.ds(u * HEADS + h, 1), :] = lse[h * HALF : (h + 1) * HALF, :].T[0:1, :]
            return 0

        lax.fori_loop(0, TOK // HALF, tile, 0)
        if last == "keep":
            outs[2 * j + 1][...] = rows_scr[...]
        elif last == "send":
            rest = rows_scr[...]
            for t in range(3):
                part = rest.astype(jnp.bfloat16)
                outs[j][ROWS + t * GROUPS : ROWS + (t + 1) * GROUPS, :] = part
                rest = rest - part.astype(jnp.float32)


def attn(deltas, shifts, kv, qs, before, last):
    n, nb = len(deltas), len(shifts)
    args = (*kv, *qs, *before)
    wide = jax.ShapeDtypeStruct((ROWS, D), jnp.float32)
    outs = {
        "state": [wide] * 3,
        "send": [jax.ShapeDtypeStruct((ROWS + 3 * GROUPS, D), jnp.bfloat16)],
        "keep": [wide, jax.ShapeDtypeStruct((GROUPS, D), jnp.float32)],
    }[last] * n
    return pl.pallas_call(
        functools.partial(attn_kernel, deltas, shifts, bool(before), last),
        out_shape=outs,
        in_specs=[VM] * len(args),
        out_specs=[VM] * len(outs),
        scratch_shapes=[
            pltpu.VMEM((nb, TOK, D), jnp.bfloat16),
            pltpu.VMEM((nb, TOK, D), jnp.bfloat16),
            pltpu.VMEM((nb, COLS, TOK), jnp.float32),
            pltpu.VMEM((COLS, D), jnp.float32),
            pltpu.VMEM((COLS, D), jnp.float32),
            pltpu.VMEM((COLS, D), jnp.float32),
            pltpu.VMEM((GROUPS, D), jnp.float32),
            pltpu.SMEM((nb, 4), jnp.int32),
        ],
        compiler_params=pltpu.CompilerParams(vmem_limit_bytes=12 * MIB),
        cost_estimate=pl.CostEstimate(
            flops=4 * ROWS * D * TOK * nb * n,
            bytes_accessed=MIB,
            transcendentals=ROWS * TOK * nb * n,
        ),
    )(*args)


def combine_kernel(a_ref, lse_ref, b_ref, c_ref, o_ref):
    x = lax.axis_index("x")

    def lse_of(ref, delta):
        terms = [
            ref[ROWS + t * GROUPS : ROWS + (t + 1) * GROUPS, :].astype(jnp.float32)
            for t in range(3)
        ]
        return jnp.where(x >= delta, terms[0] + (terms[1] + terms[2]), NEG)

    lses = (lse_ref[...], lse_of(b_ref, 1), lse_of(c_ref, 2))
    top = jnp.maximum(jnp.maximum(lses[0], lses[1]), lses[2])
    ws = [jnp.exp(lse - top) for lse in lses]
    inv = 1.0 / (ws[0] + ws[1] + ws[2])
    pad = jnp.zeros((HALF - GROUPS, D), jnp.float32)
    ws = [jnp.concatenate([w * inv, pad], axis=0).T for w in ws]
    for g in range(GROUPS):
        u, h = divmod(g, HEADS)
        rows = slice(g * HALF, (g + 1) * HALF)
        o = sum(
            ref[rows, :].astype(jnp.float32) * w[:, g : g + 1]
            for ref, w in zip((a_ref, b_ref, c_ref), ws)
        )
        o_ref[u * HALF : (u + 1) * HALF, h * D : (h + 1) * D] = o.astype(o_ref.dtype)


def combine(*args):
    return pl.pallas_call(
        combine_kernel,
        out_shape=jax.ShapeDtypeStruct((TOK, HEADS * D), jnp.bfloat16),
        in_specs=[VM] * len(args),
        out_specs=VM,
        compiler_params=pltpu.CompilerParams(vmem_limit_bytes=6 * MIB),
    )(*args)


def along(a, axis, shift, n):
    pairs = [(i, i + shift) for i in range(n)]
    if axis == "x":
        pairs = [(i, j) for i, j in pairs if 0 <= j < n]
    return lax.ppermute(a, axis, [(i, j % n) for i, j in pairs])


def local(queries, keys, values, doc_ids):
    kv, counts = prep(keys.reshape(TOK, D), values.reshape(TOK, D), doc_ids.reshape(2, D))
    q = jnp.transpose(queries.reshape(TOK // HALF, HALF, HEADS, D), (0, 2, 1, 3)).reshape(-1, D)
    q = jnp.concatenate([q, counts], axis=0)

    up1, dn1 = along(kv, "z", 1, NZ), along(kv, "z", -1, NZ)
    up2, dn2 = along(kv, "z", 2, NZ), along(kv, "z", -2, NZ)
    far = along(kv, "z", 4, NZ)
    up3, dn3 = along(up2, "z", 1, NZ), along(dn2, "z", -1, NZ)
    blocks = [kv, dn1, dn2, up1, up2, far, up3, dn3]
    q1, q2 = along(q, "x", -1, NX), along(q, "x", -2, NX)
    near = attn((2, 1), SHIFTS[:NEAR], blocks[:NEAR], [q2, q1], (), "state")
    (o2,) = attn((2,), SHIFTS[NEAR:], blocks[NEAR:], [q2], near[:3], "send")
    r2 = along(o2, "x", 2, NX)
    (o1,) = attn((1,), SHIFTS[NEAR:], blocks[NEAR:], [q1], near[3:], "send")
    r1 = along(o1, "x", 1, NX)
    o0, lse0 = attn((0,), SHIFTS, blocks, [q], (), "keep")
    merged = combine(o0, lse0, r1, r2)
    return lax.all_to_all(merged, ("y", "core"), split_axis=0, concat_axis=1, tiled=True)


def solution(mesh):
    grid = Mesh(mesh.devices.reshape(NX, NZ, 4, 2), ("x", "z", "y", "core"))
    ctx, head = ("x", "z"), ("y", "core")
    return jax.shard_map(
        local,
        mesh=grid,
        in_specs=(P(ctx, head, None), P(ctx, head, None), P(ctx, head, None), P(ctx)),
        out_specs=P(ctx + head, None),
        check_vma=False,
    )
```

```python
import functools
import math

import jax
import jax.numpy as jnp
from jax import lax
from jax.experimental import pallas as pl
from jax.experimental.pallas import tpu as pltpu
from jax.sharding import Mesh
from jax.sharding import PartitionSpec as P


TOK = 256
D = 128
HEADS = 4
NZ = 8
NX = 4
STRIPE = TOK * NZ
HALF = 128
NEG = -1e30
SHIFTS = (0, -1, -2, 1, 2, 4, 3, -3)
NEAR = 3
MIB = 1 << 20
ROWS = TOK * HEADS
GROUPS = ROWS // HALF
SCALE = D**-0.5
SCALE2 = SCALE * math.log2(math.e)
VM = pl.BlockSpec(memory_space=pltpu.VMEM)


def prep_kernel(k_ref, v_ref, ids_ref, kv_ref, cnt_ref):
    kv_ref[0:TOK, :] = k_ref[...]
    kv_ref[TOK : 2 * TOK, :] = v_ref[...]
    ids = ids_ref[...]
    row = lax.broadcasted_iota(jnp.int32, (8, D), 0)
    cnt = jnp.zeros((8, D), jnp.float32)
    for d in (1, 2, 3):
        n = jnp.sum(jnp.where(ids < d, 1.0, 0.0))
        cnt = jnp.where(row == d, n, cnt)
    cnt = cnt.astype(jnp.bfloat16)
    kv_ref[2 * TOK : 2 * TOK + 8, :] = cnt
    cnt_ref[...] = cnt


def prep(k, v, ids):
    return pl.pallas_call(
        prep_kernel,
        out_shape=[
            jax.ShapeDtypeStruct((2 * TOK + 8, D), jnp.bfloat16),
            jax.ShapeDtypeStruct((8, D), jnp.bfloat16),
        ],
        in_specs=[VM] * 3,
        out_specs=[VM] * 2,
        compiler_params=pltpu.CompilerParams(vmem_limit_bytes=4 * MIB),
    )(k, v, ids)


def attn_kernel(deltas, shifts, merge, last, *refs):
    n, nb = len(deltas), len(shifts)
    kv, refs = refs[:nb], refs[nb:]
    qs, refs = refs[:n], refs[n:]
    before, refs = (refs[: 3 * n], refs[3 * n :]) if merge else (None, refs)
    per = {"state": 3, "send": 1, "keep": 2}[last]
    outs, (kscr, vscr, sscr, acc, mscr, lscr, rows_scr, cscr) = refs[: per * n], refs[per * n :]
    x, z = lax.axis_index("x"), lax.axis_index("z")
    for i, ref in enumerate(kv):
        kscr[i] = ref[0:TOK, :]
        vscr[i] = ref[TOK : 2 * TOK, :]
        cnt = ref[2 * TOK : 2 * TOK + 8, :].astype(jnp.float32)
        cscr[i, 0] = lax.rem(z - shifts[i] + NZ, NZ)
        for d in (1, 2, 3):
            cscr[i, d] = jnp.max(cnt[d : d + 1, :]).astype(jnp.int32)

    for j, delta in enumerate(deltas):
        q_ref = qs[j]
        cnt = q_ref[ROWS : ROWS + 8, :].astype(jnp.float32)
        ends = [jnp.max(cnt[d : d + 1, :]).astype(jnp.int32) for d in (1, 2, 3)]

        def pick(tok, a, b, c, d, ends=ends):
            return jnp.where(
                tok >= ends[2], d, jnp.where(tok >= ends[1], c, jnp.where(tok >= ends[0], b, a))
            )

        def bounds(i, tok, delta=delta, pick=pick):
            c1, c2, c3 = cscr[i, 1], cscr[i, 2], cscr[i, 3]
            lo = pick(tok, jnp.int32(0), c1, c2, c3)
            hi = pick(tok, c1, c2, c3, jnp.int32(TOK))
            if delta == 0:
                b = cscr[i, 0]
                hi = jnp.minimum(hi, jnp.where(b < z, TOK, jnp.where(b == z, tok + 1, 0)))
            else:
                hi = jnp.where(x + delta < NX, hi, 0)
            return lo, hi

        def state(i, bounds=bounds):
            lo_a, hi_a = bounds(i, 0)
            lo_b, hi_b = bounds(i, TOK - 1)
            seen = hi_b > lo_a
            whole = (lo_b <= 0) & (hi_a >= TOK)
            return jnp.where(seen, jnp.where(whole, 2, 1), 0)

        def scores(masked, i, q_ref=q_ref, bounds=bounds):
            s = lax.dot_general(
                q_ref[0:ROWS, :],
                kscr[i],
                (((1,), (1,)), ((), ())),
                preferred_element_type=jnp.float32,
            )
            if masked:
                tok = lax.broadcasted_iota(jnp.int32, (TOK, TOK), 0)
                pos = lax.broadcasted_iota(jnp.int32, (TOK, TOK), 1)
                lo, hi = bounds(i, tok)
                seen = (pos >= lo) & (pos < hi)
                s = jnp.concatenate(
                    [jnp.where(seen, s[h * TOK : (h + 1) * TOK], NEG) for h in range(HEADS)],
                    axis=0,
                )
            sscr[i] = s
            mscr[...] = jnp.maximum(mscr[...], jnp.maximum(s[:, 0:D], s[:, D : 2 * D]))

        def first_pass(i, _, state=state, scores=scores):
            st = state(i)
            pl.when(st == 1)(lambda: scores(True, i))
            pl.when(st == 2)(lambda: scores(False, i))
            return 0

        mscr[...] = before[3 * j + 1][...] if merge else jnp.full((ROWS, D), NEG, jnp.float32)
        lax.fori_loop(0, nb, first_pass, 0)
        m = jnp.max(mscr[...], axis=1, keepdims=True)
        if merge:
            shrink = jnp.exp2((before[3 * j + 1][...] - m) * SCALE2)
            acc[...] = before[3 * j][...] * shrink
            lscr[...] = before[3 * j + 2][...] * shrink
        else:
            acc[...] = jnp.zeros_like(acc)
            lscr[...] = jnp.zeros_like(lscr)
        mscr[...] = jnp.broadcast_to(m, (ROWS, D))

        def weigh(i):
            s = sscr[i]
            top = mscr[...]
            lo = jnp.exp2((s[:, 0:D] - top) * SCALE2)
            hi = jnp.exp2((s[:, D : 2 * D] - top) * SCALE2)
            lscr[...] += lo + hi
            p = jnp.concatenate([lo.astype(jnp.bfloat16), hi.astype(jnp.bfloat16)], axis=1)
            acc[...] += jnp.dot(p, vscr[i], preferred_element_type=jnp.float32)

        def second_pass(i, _, state=state):
            pl.when(state(i) > 0)(lambda: weigh(i))
            return 0

        lax.fori_loop(0, nb, second_pass, 0)
        if last == "state":
            outs[3 * j][...] = acc[...]
            outs[3 * j + 1][...] = mscr[...]
            outs[3 * j + 2][...] = lscr[...]
            continue
        total = jnp.maximum(jnp.sum(lscr[...], axis=1, keepdims=True), 1e-30)
        outs[per * j][0:ROWS, :] = (acc[...] * (1.0 / total)).astype(outs[per * j].dtype)
        lse = jnp.broadcast_to(m * SCALE + jnp.log(total), (ROWS, D))
        for g in range(GROUPS):
            rows_scr[g : g + 1, :] = lse[g * HALF : (g + 1) * HALF, :].T[0:1, :]
        if last == "keep":
            outs[2 * j + 1][...] = rows_scr[...]
        elif last == "send":
            rest = rows_scr[...]
            for t in range(3):
                part = rest.astype(jnp.bfloat16)
                outs[j][ROWS + t * GROUPS : ROWS + (t + 1) * GROUPS, :] = part
                rest = rest - part.astype(jnp.float32)


def attn(deltas, shifts, kv, qs, before, last):
    n, nb = len(deltas), len(shifts)
    args = (*kv, *qs, *before)
    wide = jax.ShapeDtypeStruct((ROWS, D), jnp.float32)
    outs = {
        "state": [wide] * 3,
        "send": [jax.ShapeDtypeStruct((ROWS + 3 * GROUPS, D), jnp.bfloat16)],
        "keep": [wide, jax.ShapeDtypeStruct((GROUPS, D), jnp.float32)],
    }[last] * n
    return pl.pallas_call(
        functools.partial(attn_kernel, deltas, shifts, bool(before), last),
        out_shape=outs,
        in_specs=[VM] * len(args),
        out_specs=[VM] * len(outs),
        scratch_shapes=[
            pltpu.VMEM((nb, TOK, D), jnp.bfloat16),
            pltpu.VMEM((nb, TOK, D), jnp.bfloat16),
            pltpu.VMEM((nb, ROWS, TOK), jnp.float32),
            pltpu.VMEM((ROWS, D), jnp.float32),
            pltpu.VMEM((ROWS, D), jnp.float32),
            pltpu.VMEM((ROWS, D), jnp.float32),
            pltpu.VMEM((GROUPS, D), jnp.float32),
            pltpu.SMEM((nb, 4), jnp.int32),
        ],
        compiler_params=pltpu.CompilerParams(vmem_limit_bytes=20 * MIB),
        cost_estimate=pl.CostEstimate(
            flops=4 * ROWS * D * TOK * nb * n,
            bytes_accessed=MIB,
            transcendentals=ROWS * TOK * nb * n,
        ),
    )(*args)


def combine_kernel(a_ref, lse_ref, b_ref, c_ref, o_ref):
    x = lax.axis_index("x")

    def lse_of(ref, delta):
        terms = [
            ref[ROWS + t * GROUPS : ROWS + (t + 1) * GROUPS, :].astype(jnp.float32)
            for t in range(3)
        ]
        return jnp.where(x >= delta, terms[0] + (terms[1] + terms[2]), NEG)

    lses = (lse_ref[...], lse_of(b_ref, 1), lse_of(c_ref, 2))
    top = jnp.maximum(jnp.maximum(lses[0], lses[1]), lses[2])
    ws = [jnp.exp(lse - top) for lse in lses]
    inv = 1.0 / (ws[0] + ws[1] + ws[2])
    pad = jnp.zeros((HALF - GROUPS, D), jnp.float32)
    ws = [jnp.concatenate([w * inv, pad], axis=0).T for w in ws]
    for g in range(GROUPS):
        h, u = divmod(g, TOK // HALF)
        rows = slice(g * HALF, (g + 1) * HALF)
        o = sum(
            ref[rows, :].astype(jnp.float32) * w[:, g : g + 1]
            for ref, w in zip((a_ref, b_ref, c_ref), ws)
        )
        o_ref[u * HALF : (u + 1) * HALF, h * D : (h + 1) * D] = o.astype(o_ref.dtype)


def combine(*args):
    return pl.pallas_call(
        combine_kernel,
        out_shape=jax.ShapeDtypeStruct((TOK, HEADS * D), jnp.bfloat16),
        in_specs=[VM] * len(args),
        out_specs=VM,
        compiler_params=pltpu.CompilerParams(vmem_limit_bytes=6 * MIB),
    )(*args)


def along(a, axis, shift, n):
    pairs = [(i, i + shift) for i in range(n)]
    if axis == "x":
        pairs = [(i, j) for i, j in pairs if 0 <= j < n]
    return lax.ppermute(a, axis, [(i, j % n) for i, j in pairs])


def local(queries, keys, values, doc_ids):
    kv, counts = prep(keys.reshape(TOK, D), values.reshape(TOK, D), doc_ids.reshape(2, D))
    q = jnp.transpose(queries, (1, 0, 2)).reshape(ROWS, D)
    q = jnp.concatenate([q, counts], axis=0)

    up1, dn1 = along(kv, "z", 1, NZ), along(kv, "z", -1, NZ)
    up2, dn2 = along(kv, "z", 2, NZ), along(kv, "z", -2, NZ)
    far = along(kv, "z", 4, NZ)
    up3, dn3 = along(up2, "z", 1, NZ), along(dn2, "z", -1, NZ)
    blocks = [kv, dn1, dn2, up1, up2, far, up3, dn3]
    q1, q2 = along(q, "x", -1, NX), along(q, "x", -2, NX)
    near = attn((2, 1), SHIFTS[:NEAR], blocks[:NEAR], [q2, q1], (), "state")
    (o2,) = attn((2,), SHIFTS[NEAR:], blocks[NEAR:], [q2], near[:3], "send")
    r2 = along(o2, "x", 2, NX)
    (o1,) = attn((1,), SHIFTS[NEAR:], blocks[NEAR:], [q1], near[3:], "send")
    r1 = along(o1, "x", 1, NX)
    o0, lse0 = attn((0,), SHIFTS, blocks, [q], (), "keep")
    merged = combine(o0, lse0, r1, r2)
    return lax.all_to_all(merged, ("y", "core"), split_axis=0, concat_axis=1, tiled=True)


def solution(mesh):
    grid = Mesh(mesh.devices.reshape(NX, NZ, 4, 2), ("x", "z", "y", "core"))
    ctx, head = ("x", "z"), ("y", "core")
    return jax.shard_map(
        local,
        mesh=grid,
        in_specs=(P(ctx, head, None), P(ctx, head, None), P(ctx, head, None), P(ctx)),
        out_specs=P(ctx + head, None),
        check_vma=False,
    )
```

```python
import functools
import math

import jax
import jax.numpy as jnp
from jax import lax
from jax.experimental import pallas as pl
from jax.experimental.pallas import tpu as pltpu
from jax.sharding import Mesh
from jax.sharding import PartitionSpec as P


TOK = 256
D = 128
HEADS = 4
NZ = 8
NX = 4
HALF = 128
NEG = -1e30
SHIFTS = (0, 2, -2, 4, 1, -1, 3, -3)
NEAR = 3
MIB = 1 << 20
ROWS = TOK * HEADS
GROUPS = ROWS // HALF
SCALE = D**-0.5
SCALE2 = SCALE * math.log2(math.e)
VM = pl.BlockSpec(memory_space=pltpu.VMEM)


def prep_kernel(k_ref, v_ref, ids_ref, kv_ref, cnt_ref):
    kv_ref[0:TOK, :] = k_ref[...]
    kv_ref[TOK : 2 * TOK, :] = v_ref[...]
    ids = ids_ref[...]
    row = lax.broadcasted_iota(jnp.int32, (8, D), 0)
    cnt = jnp.zeros((8, D), jnp.float32)
    for d in (1, 2, 3):
        n = jnp.sum(jnp.where(ids < d, 1.0, 0.0))
        cnt = jnp.where(row == d, n, cnt)
    cnt = cnt.astype(jnp.bfloat16)
    kv_ref[2 * TOK : 2 * TOK + 8, :] = cnt
    cnt_ref[...] = cnt


def prep(k, v, ids):
    return pl.pallas_call(
        prep_kernel,
        out_shape=[
            jax.ShapeDtypeStruct((2 * TOK + 8, D), jnp.bfloat16),
            jax.ShapeDtypeStruct((8, D), jnp.bfloat16),
        ],
        in_specs=[VM] * 3,
        out_specs=[VM] * 2,
        compiler_params=pltpu.CompilerParams(vmem_limit_bytes=4 * MIB),
    )(k, v, ids)


def attn_kernel(deltas, shifts, merge, last, *refs):
    n, nb = len(deltas), len(shifts)
    kv, refs = refs[:nb], refs[nb:]
    qs, refs = refs[:n], refs[n:]
    before, refs = (refs[: 3 * n], refs[3 * n :]) if merge else (None, refs)
    per = {"state": 3, "send": 1, "keep": 2}[last]
    outs, (kscr, vscr, sscr, acc, mscr, lscr, rows_scr, cscr) = refs[: per * n], refs[per * n :]
    x, z = lax.axis_index("x"), lax.axis_index("z")
    for i, ref in enumerate(kv):
        kscr[i] = ref[0:TOK, :]
        vscr[i] = ref[TOK : 2 * TOK, :]
        cnt = ref[2 * TOK : 2 * TOK + 8, :].astype(jnp.float32)
        cscr[i, 0] = lax.rem(z - shifts[i] + NZ, NZ)
        for d in (1, 2, 3):
            cscr[i, d] = jnp.max(cnt[d : d + 1, :]).astype(jnp.int32)

    for j, delta in enumerate(deltas):
        q_ref = qs[j]
        cnt = q_ref[ROWS : ROWS + 8, :].astype(jnp.float32)
        ends = [jnp.max(cnt[d : d + 1, :]).astype(jnp.int32) for d in (1, 2, 3)]

        def pick(tok, a, b, c, d, ends=ends):
            return jnp.where(
                tok >= ends[2], d, jnp.where(tok >= ends[1], c, jnp.where(tok >= ends[0], b, a))
            )

        def bounds(i, tok, delta=delta, pick=pick):
            c1, c2, c3 = cscr[i, 1], cscr[i, 2], cscr[i, 3]
            lo = pick(tok, jnp.int32(0), c1, c2, c3)
            hi = pick(tok, c1, c2, c3, jnp.int32(TOK))
            if delta == 0:
                b = cscr[i, 0]
                hi = jnp.minimum(hi, jnp.where(b < z, TOK, jnp.where(b == z, tok + 1, 0)))
            else:
                hi = jnp.where(x + delta < NX, hi, 0)
            return lo, hi

        def state(i, bounds=bounds):
            lo_a, hi_a = bounds(i, 0)
            lo_b, hi_b = bounds(i, TOK - 1)
            seen = hi_b > lo_a
            whole = (lo_b <= 0) & (hi_a >= TOK)
            return jnp.where(seen, jnp.where(whole, 2, 1), 0)

        def scores(masked, i, q_ref=q_ref, bounds=bounds):
            s = lax.dot_general(
                q_ref[0:ROWS, :],
                kscr[i],
                (((1,), (1,)), ((), ())),
                preferred_element_type=jnp.float32,
            )
            if masked:
                tok = lax.broadcasted_iota(jnp.int32, (TOK, TOK), 0)
                pos = lax.broadcasted_iota(jnp.int32, (TOK, TOK), 1)
                lo, hi = bounds(i, tok)
                seen = (pos >= lo) & (pos < hi)
                s = jnp.concatenate(
                    [jnp.where(seen, s[h * TOK : (h + 1) * TOK], NEG) for h in range(HEADS)],
                    axis=0,
                )
            sscr[i] = s
            mscr[...] = jnp.maximum(mscr[...], jnp.maximum(s[:, 0:D], s[:, D : 2 * D]))

        def first_pass(i, _, state=state, scores=scores):
            st = state(i)
            pl.when(st == 1)(lambda: scores(True, i))
            pl.when(st == 2)(lambda: scores(False, i))
            return 0

        mscr[...] = before[3 * j + 1][...] if merge else jnp.full((ROWS, D), NEG, jnp.float32)
        lax.fori_loop(0, nb, first_pass, 0)
        m = jnp.max(mscr[...], axis=1, keepdims=True)
        if merge:
            shrink = jnp.exp2((before[3 * j + 1][...] - m) * SCALE2)
            acc[...] = before[3 * j][...] * shrink
            lscr[...] = before[3 * j + 2][...] * shrink
        else:
            acc[...] = jnp.zeros_like(acc)
            lscr[...] = jnp.zeros_like(lscr)
        mscr[...] = jnp.broadcast_to(m, (ROWS, D))

        def weigh(i):
            s = sscr[i]
            top = mscr[...]
            lo = jnp.exp2((s[:, 0:D] - top) * SCALE2)
            hi = jnp.exp2((s[:, D : 2 * D] - top) * SCALE2)
            lscr[...] += lo + hi
            p = jnp.concatenate([lo.astype(jnp.bfloat16), hi.astype(jnp.bfloat16)], axis=1)
            acc[...] += jnp.dot(p, vscr[i], preferred_element_type=jnp.float32)

        def second_pass(i, _, state=state):
            pl.when(state(i) > 0)(lambda: weigh(i))
            return 0

        lax.fori_loop(0, nb, second_pass, 0)
        if last == "state":
            outs[3 * j][...] = acc[...]
            outs[3 * j + 1][...] = mscr[...]
            outs[3 * j + 2][...] = lscr[...]
            continue
        total = jnp.maximum(jnp.sum(lscr[...], axis=1, keepdims=True), 1e-30)
        outs[per * j][0:ROWS, :] = (acc[...] * (1.0 / total)).astype(outs[per * j].dtype)
        lse = jnp.broadcast_to(m * SCALE + jnp.log(total), (ROWS, D))
        for g in range(GROUPS):
            rows_scr[g : g + 1, :] = lse[g * HALF : (g + 1) * HALF, :].T[0:1, :]
        if last == "keep":
            outs[2 * j + 1][...] = rows_scr[...]
        elif last == "send":
            rest = rows_scr[...]
            for t in range(3):
                part = rest.astype(jnp.bfloat16)
                outs[j][ROWS + t * GROUPS : ROWS + (t + 1) * GROUPS, :] = part
                rest = rest - part.astype(jnp.float32)


def attn(deltas, shifts, kv, qs, before, last):
    n, nb = len(deltas), len(shifts)
    args = (*kv, *qs, *before)
    wide = jax.ShapeDtypeStruct((ROWS, D), jnp.float32)
    outs = {
        "state": [wide] * 3,
        "send": [jax.ShapeDtypeStruct((ROWS + 3 * GROUPS, D), jnp.bfloat16)],
        "keep": [wide, jax.ShapeDtypeStruct((GROUPS, D), jnp.float32)],
    }[last] * n
    return pl.pallas_call(
        functools.partial(attn_kernel, deltas, shifts, bool(before), last),
        out_shape=outs,
        in_specs=[VM] * len(args),
        out_specs=[VM] * len(outs),
        scratch_shapes=[
            pltpu.VMEM((nb, TOK, D), jnp.bfloat16),
            pltpu.VMEM((nb, TOK, D), jnp.bfloat16),
            pltpu.VMEM((nb, ROWS, TOK), jnp.float32),
            pltpu.VMEM((ROWS, D), jnp.float32),
            pltpu.VMEM((ROWS, D), jnp.float32),
            pltpu.VMEM((ROWS, D), jnp.float32),
            pltpu.VMEM((GROUPS, D), jnp.float32),
            pltpu.SMEM((nb, 4), jnp.int32),
        ],
        compiler_params=pltpu.CompilerParams(vmem_limit_bytes=20 * MIB),
        cost_estimate=pl.CostEstimate(
            flops=4 * ROWS * D * TOK * nb * n,
            bytes_accessed=MIB,
            transcendentals=ROWS * TOK * nb * n,
        ),
    )(*args)


def combine_kernel(a_ref, lse_ref, b_ref, c_ref, o_ref):
    x = lax.axis_index("x")

    def lse_of(ref, delta):
        terms = [
            ref[ROWS + t * GROUPS : ROWS + (t + 1) * GROUPS, :].astype(jnp.float32)
            for t in range(3)
        ]
        return jnp.where(x >= delta, terms[0] + (terms[1] + terms[2]), NEG)

    lses = (lse_ref[...], lse_of(b_ref, 1), lse_of(c_ref, 2))
    top = jnp.maximum(jnp.maximum(lses[0], lses[1]), lses[2])
    ws = [jnp.exp(lse - top) for lse in lses]
    inv = 1.0 / (ws[0] + ws[1] + ws[2])
    pad = jnp.zeros((HALF - GROUPS, D), jnp.float32)
    ws = [jnp.concatenate([w * inv, pad], axis=0).T for w in ws]
    for g in range(GROUPS):
        h, u = divmod(g, TOK // HALF)
        rows = slice(g * HALF, (g + 1) * HALF)
        o = sum(
            ref[rows, :].astype(jnp.float32) * w[:, g : g + 1]
            for ref, w in zip((a_ref, b_ref, c_ref), ws)
        )
        o_ref[u * HALF : (u + 1) * HALF, h * D : (h + 1) * D] = o.astype(o_ref.dtype)


def combine(*args):
    return pl.pallas_call(
        combine_kernel,
        out_shape=jax.ShapeDtypeStruct((TOK, HEADS * D), jnp.bfloat16),
        in_specs=[VM] * len(args),
        out_specs=VM,
        compiler_params=pltpu.CompilerParams(vmem_limit_bytes=6 * MIB),
    )(*args)


def along(a, axis, shift, n):
    pairs = [(i, i + shift) for i in range(n)]
    if axis == "x":
        pairs = [(i, j) for i, j in pairs if 0 <= j < n]
    return lax.ppermute(a, axis, [(i, j % n) for i, j in pairs])


def local(queries, keys, values, doc_ids):
    kv, counts = prep(keys.reshape(TOK, D), values.reshape(TOK, D), doc_ids.reshape(2, D))
    q = jnp.transpose(queries, (1, 0, 2)).reshape(ROWS, D)
    q = jnp.concatenate([q, counts], axis=0)

    up2 = along(kv, "z", 2, NZ)
    dn2 = along(kv, "z", -2, NZ)
    q2 = along(q, "x", -2, NX)
    q1 = along(q, "x", -1, NX)
    far = along(kv, "z", 4, NZ)
    up3 = along(up2, "z", 1, NZ)
    dn3 = along(dn2, "z", -1, NZ)
    up1 = along(kv, "z", 1, NZ)
    dn1 = along(kv, "z", -1, NZ)
    blocks = [kv, up2, dn2, far, up1, dn1, up3, dn3]
    near = attn((2, 1), SHIFTS[:NEAR], blocks[:NEAR], [q2, q1], (), "state")
    (o2,) = attn((2,), SHIFTS[NEAR:], blocks[NEAR:], [q2], near[:3], "send")
    r2 = along(o2, "x", 2, NX)
    (o1,) = attn((1,), SHIFTS[NEAR:], blocks[NEAR:], [q1], near[3:], "send")
    r1 = along(o1, "x", 1, NX)
    o0, lse0 = attn((0,), SHIFTS, blocks, [q], (), "keep")
    merged = combine(o0, lse0, r1, r2)
    return lax.all_to_all(merged, ("y", "core"), split_axis=0, concat_axis=1, tiled=True)


def solution(mesh):
    grid = Mesh(mesh.devices.reshape(NX, NZ, 4, 2), ("x", "z", "y", "core"))
    ctx, head = ("x", "z"), ("y", "core")
    return jax.shard_map(
        local,
        mesh=grid,
        in_specs=(P(ctx, head, None), P(ctx, head, None), P(ctx, head, None), P(ctx)),
        out_specs=P(ctx + head, None),
        check_vma=False,
    )
```

```python
import functools
import math

import jax
import jax.numpy as jnp
from jax import lax
from jax.experimental import pallas as pl
from jax.experimental.pallas import tpu as pltpu
from jax.sharding import Mesh
from jax.sharding import PartitionSpec as P


TOK = 256
D = 128
HEADS = 4
NZ = 8
NX = 4
HALF = 128
NEG = -1e30
PIECE = 2 * TOK + 8
NEAR = ((0, 0, 0), (1, 0, 2), (2, 0, -2))
REST = ((0, 0, 4), (1, 0, 1), (1, PIECE, 3), (2, 0, -1), (2, PIECE, -3))
EVERY = NEAR + tuple((array + len(NEAR), row, shift) for array, row, shift in REST)
MIB = 1 << 20
ROWS = TOK * HEADS
GROUPS = ROWS // HALF
SCALE = D**-0.5
SCALE2 = SCALE * math.log2(math.e)
VM = pl.BlockSpec(memory_space=pltpu.VMEM)


def prep_kernel(k_ref, v_ref, ids_ref, kv_ref, cnt_ref, ids, sems):
    copies = [
        pltpu.make_async_copy(ids_ref, ids, sems.at[0]),
        pltpu.make_async_copy(k_ref, kv_ref.at[0:TOK, :], sems.at[1]),
        pltpu.make_async_copy(v_ref, kv_ref.at[TOK : 2 * TOK, :], sems.at[2]),
    ]
    for copy in copies:
        copy.start()
    copies[0].wait()
    row = lax.broadcasted_iota(jnp.int32, (8, D), 0)
    cnt = jnp.zeros((8, D), jnp.float32)
    for d in (1, 2, 3):
        n = jnp.sum(jnp.where(ids[...] < d, 1.0, 0.0))
        cnt = jnp.where(row == d, n, cnt)
    cnt = cnt.astype(jnp.bfloat16)
    kv_ref[2 * TOK : 2 * TOK + 8, :] = cnt
    cnt_ref[...] = cnt
    for copy in copies[1:]:
        copy.wait()


def prep(k, v, ids):
    k, v, ids = (pltpu.with_memory_space_constraint(a, pltpu.HBM) for a in (k, v, ids))
    return pl.pallas_call(
        prep_kernel,
        out_shape=[
            jax.ShapeDtypeStruct((2 * TOK + 8, D), jnp.bfloat16),
            jax.ShapeDtypeStruct((8, D), jnp.bfloat16),
        ],
        in_specs=[pl.BlockSpec(memory_space=pltpu.HBM)] * 3,
        out_specs=[VM] * 2,
        scratch_shapes=[pltpu.VMEM((2, D), jnp.int32), pltpu.SemaphoreType.DMA((3,))],
        compiler_params=pltpu.CompilerParams(vmem_limit_bytes=4 * MIB),
    )(k, v, ids)


def attn_kernel(deltas, blocks, merge, last, *refs):
    n, nb = len(deltas), len(blocks)
    arrays = 1 + max(array for array, _, _ in blocks)
    kv, refs = refs[:arrays], refs[arrays:]
    qs, refs = refs[:n], refs[n:]
    before, refs = (refs[: 3 * n], refs[3 * n :]) if merge else (None, refs)
    per = {"state": 3, "send": 1, "keep": 2}[last]
    outs, (kscr, vscr, sscr, acc, mscr, lscr, rows_scr, cscr) = refs[: per * n], refs[per * n :]
    x, z = lax.axis_index("x"), lax.axis_index("z")
    for i, (array, row, shift) in enumerate(blocks):
        ref = kv[array]
        kscr[i] = ref[row : row + TOK, :]
        vscr[i] = ref[row + TOK : row + 2 * TOK, :]
        cnt = ref[row + 2 * TOK : row + PIECE, :].astype(jnp.float32)
        cscr[i, 0] = lax.rem(z - shift + NZ, NZ)
        for d in (1, 2, 3):
            cscr[i, d] = jnp.max(cnt[d : d + 1, :]).astype(jnp.int32)

    for j, delta in enumerate(deltas):
        q_ref = qs[j]
        cnt = q_ref[ROWS : ROWS + 8, :].astype(jnp.float32)
        ends = [jnp.max(cnt[d : d + 1, :]).astype(jnp.int32) for d in (1, 2, 3)]

        def pick(tok, a, b, c, d, ends=ends):
            return jnp.where(
                tok >= ends[2], d, jnp.where(tok >= ends[1], c, jnp.where(tok >= ends[0], b, a))
            )

        def bounds(i, tok, delta=delta, pick=pick):
            c1, c2, c3 = cscr[i, 1], cscr[i, 2], cscr[i, 3]
            lo = pick(tok, jnp.int32(0), c1, c2, c3)
            hi = pick(tok, c1, c2, c3, jnp.int32(TOK))
            if delta == 0:
                b = cscr[i, 0]
                hi = jnp.minimum(hi, jnp.where(b < z, TOK, jnp.where(b == z, tok + 1, 0)))
            else:
                hi = jnp.where(x + delta < NX, hi, 0)
            return lo, hi

        def state(i, bounds=bounds):
            lo_a, hi_a = bounds(i, 0)
            lo_b, hi_b = bounds(i, TOK - 1)
            seen = hi_b > lo_a
            whole = (lo_b <= 0) & (hi_a >= TOK)
            return jnp.where(seen, jnp.where(whole, 2, 1), 0)

        def scores(masked, i, q_ref=q_ref, bounds=bounds):
            s = lax.dot_general(
                q_ref[0:ROWS, :],
                kscr[i],
                (((1,), (1,)), ((), ())),
                preferred_element_type=jnp.float32,
            )
            if masked:
                tok = lax.broadcasted_iota(jnp.int32, (TOK, TOK), 0)
                pos = lax.broadcasted_iota(jnp.int32, (TOK, TOK), 1)
                lo, hi = bounds(i, tok)
                seen = (pos >= lo) & (pos < hi)
                s = jnp.concatenate(
                    [jnp.where(seen, s[h * TOK : (h + 1) * TOK], NEG) for h in range(HEADS)],
                    axis=0,
                )
            sscr[i] = s
            mscr[...] = jnp.maximum(mscr[...], jnp.maximum(s[:, 0:D], s[:, D : 2 * D]))

        def first_pass(i, _, state=state, scores=scores):
            st = state(i)
            pl.when(st == 1)(lambda: scores(True, i))
            pl.when(st == 2)(lambda: scores(False, i))
            return 0

        mscr[...] = before[3 * j + 1][...] if merge else jnp.full((ROWS, D), NEG, jnp.float32)
        lax.fori_loop(0, nb, first_pass, 0)
        m = jnp.max(mscr[...], axis=1, keepdims=True)
        if merge:
            shrink = jnp.exp2((before[3 * j + 1][...] - m) * SCALE2)
            acc[...] = before[3 * j][...] * shrink
            lscr[...] = before[3 * j + 2][...] * shrink
        else:
            acc[...] = jnp.zeros_like(acc)
            lscr[...] = jnp.zeros_like(lscr)
        mscr[...] = jnp.broadcast_to(m, (ROWS, D))

        def weigh(i):
            s = sscr[i]
            top = mscr[...]
            lo = jnp.exp2((s[:, 0:D] - top) * SCALE2)
            hi = jnp.exp2((s[:, D : 2 * D] - top) * SCALE2)
            lscr[...] += lo + hi
            p = jnp.concatenate([lo.astype(jnp.bfloat16), hi.astype(jnp.bfloat16)], axis=1)
            acc[...] += jnp.dot(p, vscr[i], preferred_element_type=jnp.float32)

        def second_pass(i, _, state=state):
            pl.when(state(i) > 0)(lambda: weigh(i))
            return 0

        lax.fori_loop(0, nb, second_pass, 0)
        if last == "state":
            outs[3 * j][...] = acc[...]
            outs[3 * j + 1][...] = mscr[...]
            outs[3 * j + 2][...] = lscr[...]
            continue
        total = jnp.maximum(jnp.sum(lscr[...], axis=1, keepdims=True), 1e-30)
        outs[per * j][0:ROWS, :] = (acc[...] * (1.0 / total)).astype(outs[per * j].dtype)
        lse = jnp.broadcast_to(m * SCALE + jnp.log(total), (ROWS, D))
        for g in range(GROUPS):
            rows_scr[g : g + 1, :] = lse[g * HALF : (g + 1) * HALF, :].T[0:1, :]
        if last == "keep":
            outs[2 * j + 1][...] = rows_scr[...]
        elif last == "send":
            rest = rows_scr[...]
            for t in range(3):
                part = rest.astype(jnp.bfloat16)
                outs[j][ROWS + t * GROUPS : ROWS + (t + 1) * GROUPS, :] = part
                rest = rest - part.astype(jnp.float32)


def attn(deltas, blocks, kv, qs, before, last):
    n, nb = len(deltas), len(blocks)
    args = (*kv, *qs, *before)
    wide = jax.ShapeDtypeStruct((ROWS, D), jnp.float32)
    outs = {
        "state": [wide] * 3,
        "send": [jax.ShapeDtypeStruct((ROWS + 3 * GROUPS, D), jnp.bfloat16)],
        "keep": [wide, jax.ShapeDtypeStruct((GROUPS, D), jnp.float32)],
    }[last] * n
    return pl.pallas_call(
        functools.partial(attn_kernel, deltas, blocks, bool(before), last),
        out_shape=outs,
        in_specs=[VM] * len(args),
        out_specs=[VM] * len(outs),
        scratch_shapes=[
            pltpu.VMEM((nb, TOK, D), jnp.bfloat16),
            pltpu.VMEM((nb, TOK, D), jnp.bfloat16),
            pltpu.VMEM((nb, ROWS, TOK), jnp.float32),
            pltpu.VMEM((ROWS, D), jnp.float32),
            pltpu.VMEM((ROWS, D), jnp.float32),
            pltpu.VMEM((ROWS, D), jnp.float32),
            pltpu.VMEM((GROUPS, D), jnp.float32),
            pltpu.SMEM((nb, 4), jnp.int32),
        ],
        compiler_params=pltpu.CompilerParams(vmem_limit_bytes=20 * MIB),
        cost_estimate=pl.CostEstimate(
            flops=4 * ROWS * D * TOK * nb * n,
            bytes_accessed=MIB,
            transcendentals=ROWS * TOK * nb * n,
        ),
    )(*args)


def combine_kernel(a_ref, lse_ref, b_ref, c_ref, o_ref):
    x = lax.axis_index("x")

    def lse_of(ref, delta):
        terms = [
            ref[ROWS + t * GROUPS : ROWS + (t + 1) * GROUPS, :].astype(jnp.float32)
            for t in range(3)
        ]
        return jnp.where(x >= delta, terms[0] + (terms[1] + terms[2]), NEG)

    lses = (lse_ref[...], lse_of(b_ref, 1), lse_of(c_ref, 2))
    top = jnp.maximum(jnp.maximum(lses[0], lses[1]), lses[2])
    ws = [jnp.exp(lse - top) for lse in lses]
    inv = 1.0 / (ws[0] + ws[1] + ws[2])
    pad = jnp.zeros((HALF - GROUPS, D), jnp.float32)
    ws = [jnp.concatenate([w * inv, pad], axis=0).T for w in ws]
    for g in range(GROUPS):
        h, u = divmod(g, TOK // HALF)
        rows = slice(g * HALF, (g + 1) * HALF)
        o = sum(
            ref[rows, :].astype(jnp.float32) * w[:, g : g + 1]
            for ref, w in zip((a_ref, b_ref, c_ref), ws)
        )
        o_ref[u * HALF : (u + 1) * HALF, h * D : (h + 1) * D] = o.astype(o_ref.dtype)


def combine(*args):
    return pl.pallas_call(
        combine_kernel,
        out_shape=jax.ShapeDtypeStruct((TOK, HEADS * D), jnp.bfloat16),
        in_specs=[VM] * len(args),
        out_specs=VM,
        compiler_params=pltpu.CompilerParams(vmem_limit_bytes=6 * MIB),
    )(*args)


def along(a, axis, shift, n):
    pairs = [(i, i + shift) for i in range(n)]
    if axis == "x":
        pairs = [(i, j) for i, j in pairs if 0 <= j < n]
    return lax.ppermute(a, axis, [(i, j % n) for i, j in pairs])


def local(queries, keys, values, doc_ids):
    kv, counts = prep(keys.reshape(TOK, D), values.reshape(TOK, D), doc_ids.reshape(2, D))
    q = jnp.transpose(queries, (1, 0, 2)).reshape(ROWS, D)
    q = jnp.concatenate([q, counts], axis=0)

    up2 = along(kv, "z", 2, NZ)
    dn2 = along(kv, "z", -2, NZ)
    q2 = along(q, "x", -2, NX)
    q1 = along(q, "x", -1, NX)
    far = along(kv, "z", 4, NZ)
    up13 = along(jnp.concatenate([kv, up2], axis=0), "z", 1, NZ)
    dn13 = along(jnp.concatenate([kv, dn2], axis=0), "z", -1, NZ)
    first, rest = [kv, up2, dn2], [far, up13, dn13]
    near = attn((1, 2), NEAR, first, [q1, q2], (), "state")
    (o1,) = attn((1,), REST, rest, [q1], near[:3], "send")
    r1 = along(o1, "x", 1, NX)
    (o2,) = attn((2,), REST, rest, [q2], near[3:], "send")
    r2 = along(o2, "x", 2, NX)
    o0, lse0 = attn((0,), EVERY, first + rest, [q], (), "keep")
    merged = combine(o0, lse0, r1, r2)
    return lax.all_to_all(merged, ("y", "core"), split_axis=0, concat_axis=1, tiled=True)


def solution(mesh):
    grid = Mesh(mesh.devices.reshape(NX, NZ, 4, 2), ("x", "z", "y", "core"))
    ctx, head = ("x", "z"), ("y", "core")
    return jax.shard_map(
        local,
        mesh=grid,
        in_specs=(P(ctx, head, None), P(ctx, head, None), P(ctx, head, None), P(ctx)),
        out_specs=P(ctx + head, None),
        check_vma=False,
    )
```

```python
import functools
import math

import jax
import jax.numpy as jnp
from jax import lax
from jax.experimental import pallas as pl
from jax.experimental.pallas import tpu as pltpu
from jax.sharding import Mesh
from jax.sharding import PartitionSpec as P


TOK = 256
D = 128
HEADS = 4
NZ = 8
NX = 4
HALF = 128
NEG = -1e30
PIECE = 2 * TOK + 8
NEAR = ((0, 0, 0), (1, 0, 2), (2, 0, -2))
REST = ((0, 0, 4), (1, 0, 1), (1, PIECE, 3), (2, 0, -1), (2, PIECE, -3))
EVERY = NEAR + tuple((array + len(NEAR), row, shift) for array, row, shift in REST)
MIB = 1 << 20
ROWS = TOK * HEADS
GROUPS = ROWS // HALF
SCALE = D**-0.5
SCALE2 = SCALE * math.log2(math.e)
VM = pl.BlockSpec(memory_space=pltpu.VMEM)


def prep_kernel(k_ref, v_ref, ids_ref, kv_ref, cnt_ref, ids, sems):
    copies = [
        pltpu.make_async_copy(ids_ref, ids, sems.at[0]),
        pltpu.make_async_copy(k_ref, kv_ref.at[0:TOK, :], sems.at[1]),
        pltpu.make_async_copy(v_ref, kv_ref.at[TOK : 2 * TOK, :], sems.at[2]),
    ]
    for copy in copies:
        copy.start()
    copies[0].wait()
    row = lax.broadcasted_iota(jnp.int32, (8, D), 0)
    cnt = jnp.zeros((8, D), jnp.float32)
    for d in (1, 2, 3):
        n = jnp.sum(jnp.where(ids[...] < d, 1.0, 0.0))
        cnt = jnp.where(row == d, n, cnt)
    cnt = cnt.astype(jnp.bfloat16)
    kv_ref[2 * TOK : 2 * TOK + 8, :] = cnt
    cnt_ref[...] = cnt
    for copy in copies[1:]:
        copy.wait()


def prep(k, v, ids):
    k, v, ids = (pltpu.with_memory_space_constraint(a, pltpu.HBM) for a in (k, v, ids))
    return pl.pallas_call(
        prep_kernel,
        out_shape=[
            jax.ShapeDtypeStruct((2 * TOK + 8, D), jnp.bfloat16),
            jax.ShapeDtypeStruct((8, D), jnp.bfloat16),
        ],
        in_specs=[pl.BlockSpec(memory_space=pltpu.HBM)] * 3,
        out_specs=[VM] * 2,
        scratch_shapes=[pltpu.VMEM((2, D), jnp.int32), pltpu.SemaphoreType.DMA((3,))],
        compiler_params=pltpu.CompilerParams(vmem_limit_bytes=4 * MIB),
    )(k, v, ids)


def attn_kernel(deltas, blocks, merge, last, *refs):
    n, nb = len(deltas), len(blocks)
    arrays = 1 + max(array for array, _, _ in blocks)
    kv, refs = refs[:arrays], refs[arrays:]
    qs, refs = refs[:n], refs[n:]
    before, refs = (refs[: 3 * n], refs[3 * n :]) if merge else (None, refs)
    per = {"state": 3, "send": 1, "keep": 2}[last]
    outs, (kscr, vscr, sscr, acc, mscr, lscr, rows_scr, cscr) = refs[: per * n], refs[per * n :]
    x, z = lax.axis_index("x"), lax.axis_index("z")
    for i, (array, row, shift) in enumerate(blocks):
        ref = kv[array]
        kscr[i] = ref[row : row + TOK, :]
        vscr[i] = ref[row + TOK : row + 2 * TOK, :]
        cnt = ref[row + 2 * TOK : row + PIECE, :].astype(jnp.float32)
        cscr[i, 0] = lax.rem(z - shift + NZ, NZ)
        for d in (1, 2, 3):
            cscr[i, d] = jnp.max(cnt[d : d + 1, :]).astype(jnp.int32)

    for j, delta in enumerate(deltas):
        q_ref = qs[j]
        cnt = q_ref[ROWS : ROWS + 8, :].astype(jnp.float32)
        ends = [jnp.max(cnt[d : d + 1, :]).astype(jnp.int32) for d in (1, 2, 3)]

        def pick(tok, a, b, c, d, ends=ends):
            return jnp.where(
                tok >= ends[2], d, jnp.where(tok >= ends[1], c, jnp.where(tok >= ends[0], b, a))
            )

        def bounds(i, tok, delta=delta, pick=pick):
            c1, c2, c3 = cscr[i, 1], cscr[i, 2], cscr[i, 3]
            lo = pick(tok, jnp.int32(0), c1, c2, c3)
            hi = pick(tok, c1, c2, c3, jnp.int32(TOK))
            if delta == 0:
                b = cscr[i, 0]
                hi = jnp.minimum(hi, jnp.where(b < z, TOK, jnp.where(b == z, tok + 1, 0)))
            else:
                hi = jnp.where(x + delta < NX, hi, 0)
            return lo, hi

        def state(i, bounds=bounds):
            lo_a, hi_a = bounds(i, 0)
            lo_b, hi_b = bounds(i, TOK - 1)
            seen = hi_b > lo_a
            whole = (lo_b <= 0) & (hi_a >= TOK)
            return jnp.where(seen, jnp.where(whole, 2, 1), 0)

        def scores(masked, i, q_ref=q_ref, bounds=bounds):
            s = lax.dot_general(
                q_ref[0:ROWS, :],
                kscr[i],
                (((1,), (1,)), ((), ())),
                preferred_element_type=jnp.float32,
            )
            if masked:
                tok = lax.broadcasted_iota(jnp.int32, (TOK, TOK), 0)
                pos = lax.broadcasted_iota(jnp.int32, (TOK, TOK), 1)
                lo, hi = bounds(i, tok)
                seen = (pos >= lo) & (pos < hi)
                s = jnp.concatenate(
                    [jnp.where(seen, s[h * TOK : (h + 1) * TOK], NEG) for h in range(HEADS)],
                    axis=0,
                )
            sscr[i] = s
            mscr[...] = jnp.maximum(mscr[...], jnp.maximum(s[:, 0:D], s[:, D : 2 * D]))

        def first_pass(i, _, state=state, scores=scores):
            st = state(i)
            pl.when(st == 1)(lambda: scores(True, i))
            pl.when(st == 2)(lambda: scores(False, i))
            return 0

        mscr[...] = before[3 * j + 1][...] if merge else jnp.full((ROWS, D), NEG, jnp.float32)
        lax.fori_loop(0, nb, first_pass, 0)
        m = jnp.max(mscr[...], axis=1, keepdims=True)
        if merge:
            shrink = jnp.exp2((before[3 * j + 1][...] - m) * SCALE2)
            acc[...] = before[3 * j][...] * shrink
            lscr[...] = before[3 * j + 2][...] * shrink
        else:
            acc[...] = jnp.zeros_like(acc)
            lscr[...] = jnp.zeros_like(lscr)
        mscr[...] = jnp.broadcast_to(m, (ROWS, D))

        def weigh(i):
            s = sscr[i]
            top = mscr[...]
            lo = jnp.exp2((s[:, 0:D] - top) * SCALE2)
            hi = jnp.exp2((s[:, D : 2 * D] - top) * SCALE2)
            lscr[...] += lo + hi
            p = jnp.concatenate([lo.astype(jnp.bfloat16), hi.astype(jnp.bfloat16)], axis=1)
            acc[...] += jnp.dot(p, vscr[i], preferred_element_type=jnp.float32)

        def second_pass(i, _, state=state):
            pl.when(state(i) > 0)(lambda: weigh(i))
            return 0

        lax.fori_loop(0, nb, second_pass, 0)
        if last == "state":
            outs[3 * j][...] = acc[...]
            outs[3 * j + 1][...] = mscr[...]
            outs[3 * j + 2][...] = lscr[...]
            continue
        total = jnp.maximum(jnp.sum(lscr[...], axis=1, keepdims=True), 1e-30)
        outs[per * j][0:ROWS, :] = (acc[...] * (1.0 / total)).astype(outs[per * j].dtype)
        lse = jnp.broadcast_to(m * SCALE + jnp.log(total), (ROWS, D))
        for g in range(GROUPS):
            rows_scr[g : g + 1, :] = lse[g * HALF : (g + 1) * HALF, :].T[0:1, :]
        if last == "keep":
            outs[2 * j + 1][...] = rows_scr[...]
        elif last == "send":
            rest = rows_scr[...]
            for t in range(3):
                part = rest.astype(jnp.bfloat16)
                outs[j][ROWS + t * GROUPS : ROWS + (t + 1) * GROUPS, :] = part
                rest = rest - part.astype(jnp.float32)


def attn(deltas, blocks, kv, qs, before, last):
    n, nb = len(deltas), len(blocks)
    args = (*kv, *qs, *before)
    wide = jax.ShapeDtypeStruct((ROWS, D), jnp.float32)
    outs = {
        "state": [wide] * 3,
        "send": [jax.ShapeDtypeStruct((ROWS + 3 * GROUPS, D), jnp.bfloat16)],
        "keep": [wide, jax.ShapeDtypeStruct((GROUPS, D), jnp.float32)],
    }[last] * n
    return pl.pallas_call(
        functools.partial(attn_kernel, deltas, blocks, bool(before), last),
        out_shape=outs,
        in_specs=[VM] * len(args),
        out_specs=[VM] * len(outs),
        scratch_shapes=[
            pltpu.VMEM((nb, TOK, D), jnp.bfloat16),
            pltpu.VMEM((nb, TOK, D), jnp.bfloat16),
            pltpu.VMEM((nb, ROWS, TOK), jnp.float32),
            pltpu.VMEM((ROWS, D), jnp.float32),
            pltpu.VMEM((ROWS, D), jnp.float32),
            pltpu.VMEM((ROWS, D), jnp.float32),
            pltpu.VMEM((GROUPS, D), jnp.float32),
            pltpu.SMEM((nb, 4), jnp.int32),
        ],
        compiler_params=pltpu.CompilerParams(vmem_limit_bytes=20 * MIB),
        cost_estimate=pl.CostEstimate(
            flops=4 * ROWS * D * TOK * nb * n,
            bytes_accessed=MIB,
            transcendentals=ROWS * TOK * nb * n,
        ),
    )(*args)


def combine_kernel(a_ref, lse_ref, b_ref, c_ref, o_ref):
    x = lax.axis_index("x")

    def lse_of(ref, delta):
        terms = [
            ref[ROWS + t * GROUPS : ROWS + (t + 1) * GROUPS, :].astype(jnp.float32)
            for t in range(3)
        ]
        return jnp.where(x >= delta, terms[0] + (terms[1] + terms[2]), NEG)

    lses = (lse_ref[...], lse_of(b_ref, 1), lse_of(c_ref, 2))
    top = jnp.maximum(jnp.maximum(lses[0], lses[1]), lses[2])
    ws = [jnp.exp(lse - top) for lse in lses]
    inv = 1.0 / (ws[0] + ws[1] + ws[2])
    pad = jnp.zeros((HALF - GROUPS, D), jnp.float32)
    ws = [jnp.concatenate([w * inv, pad], axis=0).T for w in ws]
    for g in range(GROUPS):
        h, u = divmod(g, TOK // HALF)
        rows = slice(g * HALF, (g + 1) * HALF)
        o = sum(
            ref[rows, :].astype(jnp.float32) * w[:, g : g + 1]
            for ref, w in zip((a_ref, b_ref, c_ref), ws)
        )
        o_ref[u * HALF : (u + 1) * HALF, h * D : (h + 1) * D] = o.astype(o_ref.dtype)


def combine(*args):
    return pl.pallas_call(
        combine_kernel,
        out_shape=jax.ShapeDtypeStruct((TOK, HEADS * D), jnp.bfloat16),
        in_specs=[VM] * len(args),
        out_specs=VM,
        compiler_params=pltpu.CompilerParams(vmem_limit_bytes=6 * MIB),
    )(*args)


def along(a, axis, shift, n):
    pairs = [(i, i + shift) for i in range(n)]
    if axis == "x":
        pairs = [(i, j) for i, j in pairs if 0 <= j < n]
    return lax.ppermute(a, axis, [(i, j % n) for i, j in pairs])


def local(queries, keys, values, doc_ids):
    kv, counts = prep(keys.reshape(TOK, D), values.reshape(TOK, D), doc_ids.reshape(2, D))
    q = jnp.transpose(queries, (1, 0, 2)).reshape(ROWS, D)
    q = jnp.concatenate([q, counts], axis=0)

    up2 = along(kv, "z", 2, NZ)
    dn2 = along(kv, "z", -2, NZ)
    q2 = along(q, "x", -2, NX)
    q1 = along(q, "x", -1, NX)
    up13 = along(jnp.concatenate([kv, up2], axis=0), "z", 1, NZ)
    dn13 = along(jnp.concatenate([kv, dn2], axis=0), "z", -1, NZ)
    far = along(up2, "z", 2, NZ)
    first, rest = [kv, up2, dn2], [far, up13, dn13]
    near1 = attn((1,), NEAR, first, [q1], (), "state")
    near2 = attn((2,), NEAR, first, [q2], (), "state")
    (o1,) = attn((1,), REST, rest, [q1], near1, "send")
    r1 = along(o1, "x", 1, NX)
    (o2,) = attn((2,), REST, rest, [q2], near2, "send")
    r2 = along(o2, "x", 2, NX)
    o0, lse0 = attn((0,), EVERY, first + rest, [q], (), "keep")
    merged = combine(o0, lse0, r1, r2)
    return lax.all_to_all(merged, ("y", "core"), split_axis=0, concat_axis=1, tiled=True)


def solution(mesh):
    grid = Mesh(mesh.devices.reshape(NX, NZ, 4, 2), ("x", "z", "y", "core"))
    ctx, head = ("x", "z"), ("y", "core")
    return jax.shard_map(
        local,
        mesh=grid,
        in_specs=(P(ctx, head, None), P(ctx, head, None), P(ctx, head, None), P(ctx)),
        out_specs=P(ctx + head, None),
        check_vma=False,
    )
```

```python
import functools
import math

import jax
import jax.numpy as jnp
from jax import lax
from jax.experimental import pallas as pl
from jax.experimental.pallas import tpu as pltpu
from jax.sharding import Mesh
from jax.sharding import PartitionSpec as P


TOK = 256
D = 128
HEADS = 4
NZ = 8
NX = 4
HALF = 128
NEG = -1e30
PIECE = 2 * TOK + 8
NEAR = ((0, 0, 0, TOK, 0), (1, 0, 1, TOK, 2), (2, 0, 2, TOK, -2))
REST = (
    (0, 0, 0, TOK, 1),
    (0, PIECE, 0, PIECE + TOK, 3),
    (1, 0, 1, TOK, -1),
    (1, PIECE, 1, PIECE + TOK, -3),
    (2, 0, 3, 0, 4),
)
EVERY = NEAR + tuple((a + len(NEAR), i, b + len(NEAR), j, shift) for a, i, b, j, shift in REST)
MIB = 1 << 20
ROWS = TOK * HEADS
GROUPS = ROWS // HALF
SCALE = D**-0.5
SCALE2 = SCALE * math.log2(math.e)
VM = pl.BlockSpec(memory_space=pltpu.VMEM)


def prep_kernel(k_ref, v_ref, ids_ref, kv_ref, cnt_ref, ids, sems):
    copies = [
        pltpu.make_async_copy(ids_ref, ids, sems.at[0]),
        pltpu.make_async_copy(k_ref, kv_ref.at[0:TOK, :], sems.at[1]),
        pltpu.make_async_copy(v_ref, kv_ref.at[TOK : 2 * TOK, :], sems.at[2]),
    ]
    for copy in copies:
        copy.start()
    copies[0].wait()
    row = lax.broadcasted_iota(jnp.int32, (8, D), 0)
    cnt = jnp.zeros((8, D), jnp.float32)
    for d in (1, 2, 3):
        n = jnp.sum(jnp.where(ids[...] < d, 1.0, 0.0))
        cnt = jnp.where(row == d, n, cnt)
    cnt = cnt.astype(jnp.bfloat16)
    kv_ref[2 * TOK : 2 * TOK + 8, :] = cnt
    cnt_ref[...] = cnt
    for copy in copies[1:]:
        copy.wait()


def prep(k, v, ids):
    k, v, ids = (pltpu.with_memory_space_constraint(a, pltpu.HBM) for a in (k, v, ids))
    return pl.pallas_call(
        prep_kernel,
        out_shape=[
            jax.ShapeDtypeStruct((2 * TOK + 8, D), jnp.bfloat16),
            jax.ShapeDtypeStruct((8, D), jnp.bfloat16),
        ],
        in_specs=[pl.BlockSpec(memory_space=pltpu.HBM)] * 3,
        out_specs=[VM] * 2,
        scratch_shapes=[pltpu.VMEM((2, D), jnp.int32), pltpu.SemaphoreType.DMA((3,))],
        compiler_params=pltpu.CompilerParams(vmem_limit_bytes=4 * MIB),
    )(k, v, ids)


def attn_kernel(deltas, blocks, merge, last, *refs):
    n, nb = len(deltas), len(blocks)
    arrays = 1 + max(max(block[0], block[2]) for block in blocks)
    kv, refs = refs[:arrays], refs[arrays:]
    qs, refs = refs[:n], refs[n:]
    before, refs = (refs[: 3 * n], refs[3 * n :]) if merge else (None, refs)
    per = {"state": 3, "send": 1, "keep": 2}[last]
    outs, (kscr, vscr, sscr, acc, mscr, lscr, rows_scr, cscr) = refs[: per * n], refs[per * n :]
    x, z = lax.axis_index("x"), lax.axis_index("z")
    for i, (k_at, k_row, v_at, v_row, shift) in enumerate(blocks):
        kscr[i] = kv[k_at][k_row : k_row + TOK, :]
        vscr[i] = kv[v_at][v_row : v_row + TOK, :]
        cnt = kv[v_at][v_row + TOK : v_row + TOK + 8, :].astype(jnp.float32)
        cscr[i, 0] = lax.rem(z - shift + NZ, NZ)
        for d in (1, 2, 3):
            cscr[i, d] = jnp.max(cnt[d : d + 1, :]).astype(jnp.int32)

    for j, delta in enumerate(deltas):
        q_ref = qs[j]
        cnt = q_ref[ROWS : ROWS + 8, :].astype(jnp.float32)
        ends = [jnp.max(cnt[d : d + 1, :]).astype(jnp.int32) for d in (1, 2, 3)]

        def pick(tok, a, b, c, d, ends=ends):
            return jnp.where(
                tok >= ends[2], d, jnp.where(tok >= ends[1], c, jnp.where(tok >= ends[0], b, a))
            )

        def bounds(i, tok, delta=delta, pick=pick):
            c1, c2, c3 = cscr[i, 1], cscr[i, 2], cscr[i, 3]
            lo = pick(tok, jnp.int32(0), c1, c2, c3)
            hi = pick(tok, c1, c2, c3, jnp.int32(TOK))
            if delta == 0:
                b = cscr[i, 0]
                hi = jnp.minimum(hi, jnp.where(b < z, TOK, jnp.where(b == z, tok + 1, 0)))
            else:
                hi = jnp.where(x + delta < NX, hi, 0)
            return lo, hi

        def state(i, bounds=bounds):
            lo_a, hi_a = bounds(i, 0)
            lo_b, hi_b = bounds(i, TOK - 1)
            seen = hi_b > lo_a
            whole = (lo_b <= 0) & (hi_a >= TOK)
            return jnp.where(seen, jnp.where(whole, 2, 1), 0)

        def scores(masked, i, q_ref=q_ref, bounds=bounds):
            s = lax.dot_general(
                q_ref[0:ROWS, :],
                kscr[i],
                (((1,), (1,)), ((), ())),
                preferred_element_type=jnp.float32,
            )
            if masked:
                tok = lax.broadcasted_iota(jnp.int32, (TOK, TOK), 0)
                pos = lax.broadcasted_iota(jnp.int32, (TOK, TOK), 1)
                lo, hi = bounds(i, tok)
                seen = (pos >= lo) & (pos < hi)
                s = jnp.concatenate(
                    [jnp.where(seen, s[h * TOK : (h + 1) * TOK], NEG) for h in range(HEADS)],
                    axis=0,
                )
            sscr[i] = s
            mscr[...] = jnp.maximum(mscr[...], jnp.maximum(s[:, 0:D], s[:, D : 2 * D]))

        def first_pass(i, _, state=state, scores=scores):
            st = state(i)
            pl.when(st == 1)(lambda: scores(True, i))
            pl.when(st == 2)(lambda: scores(False, i))
            return 0

        mscr[...] = before[3 * j + 1][...] if merge else jnp.full((ROWS, D), NEG, jnp.float32)
        lax.fori_loop(0, nb, first_pass, 0)
        m = jnp.max(mscr[...], axis=1, keepdims=True)
        if merge:
            shrink = jnp.exp2((before[3 * j + 1][...] - m) * SCALE2)
            acc[...] = before[3 * j][...] * shrink
            lscr[...] = before[3 * j + 2][...] * shrink
        else:
            acc[...] = jnp.zeros_like(acc)
            lscr[...] = jnp.zeros_like(lscr)
        mscr[...] = jnp.broadcast_to(m, (ROWS, D))

        def weigh(i):
            s = sscr[i]
            top = mscr[...]
            lo = jnp.exp2((s[:, 0:D] - top) * SCALE2)
            hi = jnp.exp2((s[:, D : 2 * D] - top) * SCALE2)
            lscr[...] += lo + hi
            p = jnp.concatenate([lo.astype(jnp.bfloat16), hi.astype(jnp.bfloat16)], axis=1)
            acc[...] += jnp.dot(p, vscr[i], preferred_element_type=jnp.float32)

        def second_pass(i, _, state=state):
            pl.when(state(i) > 0)(lambda: weigh(i))
            return 0

        lax.fori_loop(0, nb, second_pass, 0)
        if last == "state":
            outs[3 * j][...] = acc[...]
            outs[3 * j + 1][...] = mscr[...]
            outs[3 * j + 2][...] = lscr[...]
            continue
        total = jnp.maximum(jnp.sum(lscr[...], axis=1, keepdims=True), 1e-30)
        outs[per * j][0:ROWS, :] = (acc[...] * (1.0 / total)).astype(outs[per * j].dtype)
        lse = jnp.broadcast_to(m * SCALE + jnp.log(total), (ROWS, D))
        for g in range(GROUPS):
            rows_scr[g : g + 1, :] = lse[g * HALF : (g + 1) * HALF, :].T[0:1, :]
        if last == "keep":
            outs[2 * j + 1][...] = rows_scr[...]
        elif last == "send":
            rest = rows_scr[...]
            for t in range(3):
                part = rest.astype(jnp.bfloat16)
                outs[j][ROWS + t * GROUPS : ROWS + (t + 1) * GROUPS, :] = part
                rest = rest - part.astype(jnp.float32)


def attn(deltas, blocks, kv, qs, before, last):
    n, nb = len(deltas), len(blocks)
    args = (*kv, *qs, *before)
    wide = jax.ShapeDtypeStruct((ROWS, D), jnp.float32)
    outs = {
        "state": [wide] * 3,
        "send": [jax.ShapeDtypeStruct((ROWS + 3 * GROUPS, D), jnp.bfloat16)],
        "keep": [wide, jax.ShapeDtypeStruct((GROUPS, D), jnp.float32)],
    }[last] * n
    return pl.pallas_call(
        functools.partial(attn_kernel, deltas, blocks, bool(before), last),
        out_shape=outs,
        in_specs=[VM] * len(args),
        out_specs=[VM] * len(outs),
        scratch_shapes=[
            pltpu.VMEM((nb, TOK, D), jnp.bfloat16),
            pltpu.VMEM((nb, TOK, D), jnp.bfloat16),
            pltpu.VMEM((nb, ROWS, TOK), jnp.float32),
            pltpu.VMEM((ROWS, D), jnp.float32),
            pltpu.VMEM((ROWS, D), jnp.float32),
            pltpu.VMEM((ROWS, D), jnp.float32),
            pltpu.VMEM((GROUPS, D), jnp.float32),
            pltpu.SMEM((nb, 4), jnp.int32),
        ],
        compiler_params=pltpu.CompilerParams(vmem_limit_bytes=20 * MIB),
        cost_estimate=pl.CostEstimate(
            flops=4 * ROWS * D * TOK * nb * n,
            bytes_accessed=MIB,
            transcendentals=ROWS * TOK * nb * n,
        ),
    )(*args)


def combine_kernel(a_ref, lse_ref, b_ref, c_ref, o_ref):
    x = lax.axis_index("x")

    def lse_of(ref, delta):
        terms = [
            ref[ROWS + t * GROUPS : ROWS + (t + 1) * GROUPS, :].astype(jnp.float32)
            for t in range(3)
        ]
        return jnp.where(x >= delta, terms[0] + (terms[1] + terms[2]), NEG)

    lses = (lse_ref[...], lse_of(b_ref, 1), lse_of(c_ref, 2))
    top = jnp.maximum(jnp.maximum(lses[0], lses[1]), lses[2])
    ws = [jnp.exp(lse - top) for lse in lses]
    inv = 1.0 / (ws[0] + ws[1] + ws[2])
    pad = jnp.zeros((HALF - GROUPS, D), jnp.float32)
    ws = [jnp.concatenate([w * inv, pad], axis=0).T for w in ws]
    for g in range(GROUPS):
        h, u = divmod(g, TOK // HALF)
        rows = slice(g * HALF, (g + 1) * HALF)
        o = sum(
            ref[rows, :].astype(jnp.float32) * w[:, g : g + 1]
            for ref, w in zip((a_ref, b_ref, c_ref), ws)
        )
        o_ref[u * HALF : (u + 1) * HALF, h * D : (h + 1) * D] = o.astype(o_ref.dtype)


def combine(*args):
    return pl.pallas_call(
        combine_kernel,
        out_shape=jax.ShapeDtypeStruct((TOK, HEADS * D), jnp.bfloat16),
        in_specs=[VM] * len(args),
        out_specs=VM,
        compiler_params=pltpu.CompilerParams(vmem_limit_bytes=6 * MIB),
    )(*args)


def along(a, axis, shift, n):
    pairs = [(i, i + shift) for i in range(n)]
    if axis == "x":
        pairs = [(i, j) for i, j in pairs if 0 <= j < n]
    return lax.ppermute(a, axis, [(i, j % n) for i, j in pairs])


def local(queries, keys, values, doc_ids):
    kv, counts = prep(keys.reshape(TOK, D), values.reshape(TOK, D), doc_ids.reshape(2, D))
    q = jnp.transpose(queries, (1, 0, 2)).reshape(ROWS, D)
    q = jnp.concatenate([q, counts], axis=0)

    up2 = along(kv, "z", 2, NZ)
    dn2 = along(kv, "z", -2, NZ)
    q2 = along(q, "x", -2, NX)
    q1 = along(q, "x", -1, NX)
    up13 = along(jnp.concatenate([kv, up2], axis=0), "z", 1, NZ)
    dn13 = along(jnp.concatenate([kv, dn2], axis=0), "z", -1, NZ)
    far_k = along(up2[0:TOK], "z", 2, NZ)
    far_v = along(dn2[TOK:PIECE], "z", -2, NZ)
    first, rest = [kv, up2, dn2], [up13, dn13, far_k, far_v]
    near1 = attn((1,), NEAR, first, [q1], (), "state")
    near2 = attn((2,), NEAR, first, [q2], (), "state")
    (o1,) = attn((1,), REST, rest, [q1], near1, "send")
    r1 = along(o1, "x", 1, NX)
    (o2,) = attn((2,), REST, rest, [q2], near2, "send")
    r2 = along(o2, "x", 2, NX)
    o0, lse0 = attn((0,), EVERY, first + rest, [q], (), "keep")
    merged = combine(o0, lse0, r1, r2)
    return lax.all_to_all(merged, ("y", "core"), split_axis=0, concat_axis=1, tiled=True)


def solution(mesh):
    grid = Mesh(mesh.devices.reshape(NX, NZ, 4, 2), ("x", "z", "y", "core"))
    ctx, head = ("x", "z"), ("y", "core")
    return jax.shard_map(
        local,
        mesh=grid,
        in_specs=(P(ctx, head, None), P(ctx, head, None), P(ctx, head, None), P(ctx)),
        out_specs=P(ctx + head, None),
        check_vma=False,
    )
```

```python
import functools
import math

import jax
import jax.numpy as jnp
from jax import lax
from jax.experimental import pallas as pl
from jax.experimental.pallas import tpu as pltpu
from jax.sharding import Mesh
from jax.sharding import PartitionSpec as P


TOK = 256
D = 128
HEADS = 4
NZ = 8
NX = 4
HALF = 128
NEG = -1e30
PIECE = 2 * TOK + 8
NEAR = ((0, 0, 0, TOK, 0), (1, 0, 1, TOK, 2), (2, 0, 2, TOK, -2))
REST = (
    (0, 0, 0, TOK, 1),
    (0, PIECE, 0, PIECE + TOK, 3),
    (1, 0, 1, TOK, -1),
    (1, PIECE, 1, PIECE + TOK, -3),
    (2, 0, 3, 0, 4),
)
EVERY = NEAR + tuple((a + len(NEAR), i, b + len(NEAR), j, shift) for a, i, b, j, shift in REST)
MIB = 1 << 20
ROWS = TOK * HEADS
GROUPS = ROWS // HALF
SCALE = D**-0.5
SCALE2 = SCALE * math.log2(math.e)
VM = pl.BlockSpec(memory_space=pltpu.VMEM)


def prep_kernel(k_ref, v_ref, q_ref, ids_ref, kv_ref, qc_ref, ids, sems):
    copies = [
        pltpu.make_async_copy(ids_ref, ids, sems.at[0]),
        pltpu.make_async_copy(k_ref, kv_ref.at[0:TOK, :], sems.at[1]),
        pltpu.make_async_copy(v_ref, kv_ref.at[TOK : 2 * TOK, :], sems.at[2]),
        pltpu.make_async_copy(q_ref, qc_ref.at[0:ROWS, :], sems.at[3]),
    ]
    for copy in copies:
        copy.start()
    copies[0].wait()
    row = lax.broadcasted_iota(jnp.int32, (8, D), 0)
    cnt = jnp.zeros((8, D), jnp.float32)
    for d in (1, 2, 3):
        n = jnp.sum(jnp.where(ids[...] < d, 1.0, 0.0))
        cnt = jnp.where(row == d, n, cnt)
    cnt = cnt.astype(jnp.bfloat16)
    kv_ref[2 * TOK : PIECE, :] = cnt
    qc_ref[ROWS : ROWS + 8, :] = cnt
    for copy in copies[1:]:
        copy.wait()


def prep(*args):
    args = [pltpu.with_memory_space_constraint(a, pltpu.HBM) for a in args]
    return pl.pallas_call(
        prep_kernel,
        out_shape=[
            jax.ShapeDtypeStruct((PIECE, D), jnp.bfloat16),
            jax.ShapeDtypeStruct((ROWS + 8, D), jnp.bfloat16),
        ],
        in_specs=[pl.BlockSpec(memory_space=pltpu.HBM)] * 4,
        out_specs=[VM] * 2,
        scratch_shapes=[pltpu.VMEM((2, D), jnp.int32), pltpu.SemaphoreType.DMA((4,))],
        compiler_params=pltpu.CompilerParams(vmem_limit_bytes=4 * MIB),
    )(*args)


def attn_kernel(deltas, blocks, merge, last, *refs):
    n, nb = len(deltas), len(blocks)
    arrays = 1 + max(max(block[0], block[2]) for block in blocks)
    kv, refs = refs[:arrays], refs[arrays:]
    qs, refs = refs[:n], refs[n:]
    before, refs = (refs[: 3 * n], refs[3 * n :]) if merge else (None, refs)
    per = {"state": 3, "send": 1, "keep": 2}[last]
    outs, (kscr, vscr, sscr, acc, mscr, lscr, rows_scr, cscr) = refs[: per * n], refs[per * n :]
    x, z = lax.axis_index("x"), lax.axis_index("z")
    for i, (k_at, k_row, v_at, v_row, shift) in enumerate(blocks):
        kscr[i] = kv[k_at][k_row : k_row + TOK, :]
        vscr[i] = kv[v_at][v_row : v_row + TOK, :]
        cnt = kv[v_at][v_row + TOK : v_row + TOK + 8, :].astype(jnp.float32)
        cscr[i, 0] = lax.rem(z - shift + NZ, NZ)
        for d in (1, 2, 3):
            cscr[i, d] = jnp.max(cnt[d : d + 1, :]).astype(jnp.int32)

    for j, delta in enumerate(deltas):
        q_ref = qs[j]
        cnt = q_ref[ROWS : ROWS + 8, :].astype(jnp.float32)
        ends = [jnp.max(cnt[d : d + 1, :]).astype(jnp.int32) for d in (1, 2, 3)]

        def pick(tok, a, b, c, d, ends=ends):
            return jnp.where(
                tok >= ends[2], d, jnp.where(tok >= ends[1], c, jnp.where(tok >= ends[0], b, a))
            )

        def bounds(i, tok, delta=delta, pick=pick):
            c1, c2, c3 = cscr[i, 1], cscr[i, 2], cscr[i, 3]
            lo = pick(tok, jnp.int32(0), c1, c2, c3)
            hi = pick(tok, c1, c2, c3, jnp.int32(TOK))
            if delta == 0:
                b = cscr[i, 0]
                hi = jnp.minimum(hi, jnp.where(b < z, TOK, jnp.where(b == z, tok + 1, 0)))
            else:
                hi = jnp.where(x + delta < NX, hi, 0)
            return lo, hi

        def state(i, bounds=bounds):
            lo_a, hi_a = bounds(i, 0)
            lo_b, hi_b = bounds(i, TOK - 1)
            seen = hi_b > lo_a
            whole = (lo_b <= 0) & (hi_a >= TOK)
            return jnp.where(seen, jnp.where(whole, 2, 1), 0)

        def scores(masked, i, q_ref=q_ref, bounds=bounds):
            s = lax.dot_general(
                q_ref[0:ROWS, :],
                kscr[i],
                (((1,), (1,)), ((), ())),
                preferred_element_type=jnp.float32,
            )
            if masked:
                tok = lax.broadcasted_iota(jnp.int32, (ROWS, D), 0) >> 2
                pos = lax.broadcasted_iota(jnp.int32, (ROWS, D), 1)
                lo, hi = bounds(i, tok)
                halves = [
                    jnp.where((pos + c >= lo) & (pos + c < hi), s[:, c : c + D], NEG)
                    for c in range(0, TOK, D)
                ]
                s = jnp.concatenate(halves, axis=1)
            sscr[i] = s
            mscr[...] = jnp.maximum(mscr[...], jnp.maximum(s[:, 0:D], s[:, D : 2 * D]))

        def first_pass(i, _, state=state, scores=scores):
            st = state(i)
            pl.when(st == 1)(lambda: scores(True, i))
            pl.when(st == 2)(lambda: scores(False, i))
            return 0

        mscr[...] = before[3 * j + 1][...] if merge else jnp.full((ROWS, D), NEG, jnp.float32)
        lax.fori_loop(0, nb, first_pass, 0)
        m = jnp.max(mscr[...], axis=1, keepdims=True)
        if merge:
            shrink = jnp.exp2((before[3 * j + 1][...] - m) * SCALE2)
            acc[...] = before[3 * j][...] * shrink
            lscr[...] = before[3 * j + 2][...] * shrink
        else:
            acc[...] = jnp.zeros_like(acc)
            lscr[...] = jnp.zeros_like(lscr)
        mscr[...] = jnp.broadcast_to(m, (ROWS, D))

        def weigh(i):
            s = sscr[i]
            top = mscr[...]
            lo = jnp.exp2((s[:, 0:D] - top) * SCALE2)
            hi = jnp.exp2((s[:, D : 2 * D] - top) * SCALE2)
            lscr[...] += lo + hi
            p = jnp.concatenate([lo.astype(jnp.bfloat16), hi.astype(jnp.bfloat16)], axis=1)
            acc[...] += jnp.dot(p, vscr[i], preferred_element_type=jnp.float32)

        def second_pass(i, _, state=state):
            pl.when(state(i) > 0)(lambda: weigh(i))
            return 0

        lax.fori_loop(0, nb, second_pass, 0)
        if last == "state":
            outs[3 * j][...] = acc[...]
            outs[3 * j + 1][...] = mscr[...]
            outs[3 * j + 2][...] = lscr[...]
            continue
        total = jnp.maximum(jnp.sum(lscr[...], axis=1, keepdims=True), 1e-30)
        outs[per * j][0:ROWS, :] = (acc[...] * (1.0 / total)).astype(outs[per * j].dtype)
        lse = jnp.broadcast_to(m * SCALE + jnp.log(total), (ROWS, D))
        for g in range(GROUPS):
            rows_scr[g : g + 1, :] = lse[g * HALF : (g + 1) * HALF, :].T[0:1, :]
        if last == "keep":
            outs[2 * j + 1][...] = rows_scr[...]
        elif last == "send":
            rest = rows_scr[...]
            for t in range(3):
                part = rest.astype(jnp.bfloat16)
                outs[j][ROWS + t * GROUPS : ROWS + (t + 1) * GROUPS, :] = part
                rest = rest - part.astype(jnp.float32)


def attn(deltas, blocks, kv, qs, before, last):
    n, nb = len(deltas), len(blocks)
    args = (*kv, *qs, *before)
    wide = jax.ShapeDtypeStruct((ROWS, D), jnp.float32)
    outs = {
        "state": [wide] * 3,
        "send": [jax.ShapeDtypeStruct((ROWS + 3 * GROUPS, D), jnp.bfloat16)],
        "keep": [wide, jax.ShapeDtypeStruct((GROUPS, D), jnp.float32)],
    }[last] * n
    return pl.pallas_call(
        functools.partial(attn_kernel, deltas, blocks, bool(before), last),
        out_shape=outs,
        in_specs=[VM] * len(args),
        out_specs=[VM] * len(outs),
        scratch_shapes=[
            pltpu.VMEM((nb, TOK, D), jnp.bfloat16),
            pltpu.VMEM((nb, TOK, D), jnp.bfloat16),
            pltpu.VMEM((nb, ROWS, TOK), jnp.float32),
            pltpu.VMEM((ROWS, D), jnp.float32),
            pltpu.VMEM((ROWS, D), jnp.float32),
            pltpu.VMEM((ROWS, D), jnp.float32),
            pltpu.VMEM((GROUPS, D), jnp.float32),
            pltpu.SMEM((nb, 4), jnp.int32),
        ],
        compiler_params=pltpu.CompilerParams(vmem_limit_bytes=20 * MIB),
        cost_estimate=pl.CostEstimate(
            flops=4 * ROWS * D * TOK * nb * n,
            bytes_accessed=MIB,
            transcendentals=ROWS * TOK * nb * n,
        ),
    )(*args)


def combine_kernel(a_ref, lse_ref, b_ref, c_ref, o_ref, scr):
    x = lax.axis_index("x")

    def lse_of(ref, delta):
        terms = [
            ref[ROWS + t * GROUPS : ROWS + (t + 1) * GROUPS, :].astype(jnp.float32)
            for t in range(3)
        ]
        return jnp.where(x >= delta, terms[0] + (terms[1] + terms[2]), NEG)

    lses = (lse_ref[...], lse_of(b_ref, 1), lse_of(c_ref, 2))
    top = jnp.maximum(jnp.maximum(lses[0], lses[1]), lses[2])
    ws = [jnp.exp(lse - top) for lse in lses]
    inv = 1.0 / (ws[0] + ws[1] + ws[2])
    pad = jnp.zeros((HALF - GROUPS, D), jnp.float32)
    ws = [jnp.concatenate([w * inv, pad], axis=0).T for w in ws]
    for g in range(GROUPS):
        rows = slice(g * HALF, (g + 1) * HALF)
        scr[rows, :] = sum(
            ref[rows, :].astype(jnp.float32) * w[:, g : g + 1]
            for ref, w in zip((a_ref, b_ref, c_ref), ws)
        )
    for h in range(HEADS):
        rows = pl.ds(h, TOK, stride=HEADS)
        o_ref[:, h * D : (h + 1) * D] = scr[rows, :].astype(o_ref.dtype)


def combine(*args):
    return pl.pallas_call(
        combine_kernel,
        out_shape=jax.ShapeDtypeStruct((TOK, HEADS * D), jnp.bfloat16),
        in_specs=[VM] * len(args),
        out_specs=VM,
        scratch_shapes=[pltpu.VMEM((ROWS, D), jnp.float32)],
        compiler_params=pltpu.CompilerParams(vmem_limit_bytes=6 * MIB),
    )(*args)


def along(a, axis, shift, n):
    pairs = [(i, i + shift) for i in range(n)]
    if axis == "x":
        pairs = [(i, j) for i, j in pairs if 0 <= j < n]
    return lax.ppermute(a, axis, [(i, j % n) for i, j in pairs])


def local(queries, keys, values, doc_ids):
    kv, q = prep(
        keys.reshape(TOK, D), values.reshape(TOK, D), queries.reshape(ROWS, D), doc_ids.reshape(2, D)
    )
    up2 = along(kv, "z", 2, NZ)
    dn2 = along(kv, "z", -2, NZ)
    q2 = along(q, "x", -2, NX)
    q1 = along(q, "x", -1, NX)
    up13 = along(jnp.concatenate([kv, up2], axis=0), "z", 1, NZ)
    dn13 = along(jnp.concatenate([kv, dn2], axis=0), "z", -1, NZ)
    far_k = along(up2[0:TOK], "z", 2, NZ)
    far_v = along(dn2[TOK:PIECE], "z", -2, NZ)
    first, rest = [kv, up2, dn2], [up13, dn13, far_k, far_v]
    near1 = attn((1,), NEAR, first, [q1], (), "state")
    near2 = attn((2,), NEAR, first, [q2], (), "state")
    (o1,) = attn((1,), REST, rest, [q1], near1, "send")
    r1 = along(o1, "x", 1, NX)
    (o2,) = attn((2,), REST, rest, [q2], near2, "send")
    r2 = along(o2, "x", 2, NX)
    o0, lse0 = attn((0,), EVERY, first + rest, [q], (), "keep")
    merged = combine(o0, lse0, r1, r2)
    return lax.all_to_all(merged, ("y", "core"), split_axis=0, concat_axis=1, tiled=True)


def solution(mesh):
    grid = Mesh(mesh.devices.reshape(NX, NZ, 4, 2), ("x", "z", "y", "core"))
    ctx, head = ("x", "z"), ("y", "core")
    return jax.shard_map(
        local,
        mesh=grid,
        in_specs=(P(ctx, head, None), P(ctx, head, None), P(ctx, head, None), P(ctx)),
        out_specs=P(ctx + head, None),
        check_vma=False,
    )
```

```python
import functools
import math

import jax
import jax.numpy as jnp
from jax import lax
from jax.experimental import pallas as pl
from jax.experimental.pallas import tpu as pltpu
from jax.sharding import Mesh
from jax.sharding import PartitionSpec as P


TOK = 256
D = 128
HEADS = 4
NZ = 8
NX = 4
HALF = 128
NEG = -1e30
PIECE = 2 * TOK + 8
NEAR = ((0, 0, 0, TOK, 0), (1, 0, 1, TOK, 2), (2, 0, 2, TOK, -2))
MID = (
    (0, 0, 0, TOK, 1),
    (0, PIECE, 0, PIECE + TOK, 3),
    (1, 0, 1, TOK, -1),
    (1, PIECE, 1, PIECE + TOK, -3),
)
LAST = ((0, 0, 1, 0, 4),)


def moved(blocks, by):
    return tuple((a + by, i, b + by, j, shift) for a, i, b, j, shift in blocks)


EVERY = NEAR + moved(MID, 3) + moved(LAST, 5)
MIB = 1 << 20
ROWS = TOK * HEADS
GROUPS = ROWS // HALF
SCALE = D**-0.5
SCALE2 = SCALE * math.log2(math.e)
VM = pl.BlockSpec(memory_space=pltpu.VMEM)


def prep_kernel(k_ref, v_ref, q_ref, ids_ref, kv_ref, qc_ref, ids, sems):
    copies = [
        pltpu.make_async_copy(ids_ref, ids, sems.at[0]),
        pltpu.make_async_copy(k_ref, kv_ref.at[0:TOK, :], sems.at[1]),
        pltpu.make_async_copy(v_ref, kv_ref.at[TOK : 2 * TOK, :], sems.at[2]),
        pltpu.make_async_copy(q_ref, qc_ref.at[0:ROWS, :], sems.at[3]),
    ]
    for copy in copies:
        copy.start()
    copies[0].wait()
    row = lax.broadcasted_iota(jnp.int32, (8, D), 0)
    cnt = jnp.zeros((8, D), jnp.float32)
    for d in (1, 2, 3):
        n = jnp.sum(jnp.where(ids[...] < d, 1.0, 0.0))
        cnt = jnp.where(row == d, n, cnt)
    cnt = cnt.astype(jnp.bfloat16)
    kv_ref[2 * TOK : PIECE, :] = cnt
    qc_ref[ROWS : ROWS + 8, :] = cnt
    for copy in copies[1:]:
        copy.wait()


def prep(*args):
    args = [pltpu.with_memory_space_constraint(a, pltpu.HBM) for a in args]
    return pl.pallas_call(
        prep_kernel,
        out_shape=[
            jax.ShapeDtypeStruct((PIECE, D), jnp.bfloat16),
            jax.ShapeDtypeStruct((ROWS + 8, D), jnp.bfloat16),
        ],
        in_specs=[pl.BlockSpec(memory_space=pltpu.HBM)] * 4,
        out_specs=[VM] * 2,
        scratch_shapes=[pltpu.VMEM((2, D), jnp.int32), pltpu.SemaphoreType.DMA((4,))],
        compiler_params=pltpu.CompilerParams(vmem_limit_bytes=4 * MIB),
    )(*args)


def attn_kernel(deltas, blocks, merge, last, *refs):
    n, nb = len(deltas), len(blocks)
    arrays = 1 + max(max(block[0], block[2]) for block in blocks)
    kv, refs = refs[:arrays], refs[arrays:]
    qs, refs = refs[:n], refs[n:]
    before, refs = (refs[: 3 * n], refs[3 * n :]) if merge else (None, refs)
    per = {"state": 3, "send": 1, "keep": 2}[last]
    outs, (kscr, vscr, sscr, acc, mscr, lscr, rows_scr, cscr) = refs[: per * n], refs[per * n :]
    x, z = lax.axis_index("x"), lax.axis_index("z")
    for i, (k_at, k_row, v_at, v_row, shift) in enumerate(blocks):
        kscr[i] = kv[k_at][k_row : k_row + TOK, :]
        vscr[i] = kv[v_at][v_row : v_row + TOK, :]
        cnt = kv[v_at][v_row + TOK : v_row + TOK + 8, :].astype(jnp.float32)
        cscr[i, 0] = lax.rem(z - shift + NZ, NZ)
        for d in (1, 2, 3):
            cscr[i, d] = jnp.max(cnt[d : d + 1, :]).astype(jnp.int32)

    for j, delta in enumerate(deltas):
        q_ref = qs[j]
        cnt = q_ref[ROWS : ROWS + 8, :].astype(jnp.float32)
        ends = [jnp.max(cnt[d : d + 1, :]).astype(jnp.int32) for d in (1, 2, 3)]

        def pick(tok, a, b, c, d, ends=ends):
            return jnp.where(
                tok >= ends[2], d, jnp.where(tok >= ends[1], c, jnp.where(tok >= ends[0], b, a))
            )

        def bounds(i, tok, delta=delta, pick=pick):
            c1, c2, c3 = cscr[i, 1], cscr[i, 2], cscr[i, 3]
            lo = pick(tok, jnp.int32(0), c1, c2, c3)
            hi = pick(tok, c1, c2, c3, jnp.int32(TOK))
            if delta == 0:
                b = cscr[i, 0]
                hi = jnp.minimum(hi, jnp.where(b < z, TOK, jnp.where(b == z, tok + 1, 0)))
            else:
                hi = jnp.where(x + delta < NX, hi, 0)
            return lo, hi

        def state(i, bounds=bounds):
            lo_a, hi_a = bounds(i, 0)
            lo_b, hi_b = bounds(i, TOK - 1)
            seen = hi_b > lo_a
            whole = (lo_b <= 0) & (hi_a >= TOK)
            return jnp.where(seen, jnp.where(whole, 2, 1), 0)

        def scores(masked, i, q_ref=q_ref, bounds=bounds):
            s = lax.dot_general(
                q_ref[0:ROWS, :],
                kscr[i],
                (((1,), (1,)), ((), ())),
                preferred_element_type=jnp.float32,
            )
            if masked:
                tok = lax.broadcasted_iota(jnp.int32, (ROWS, D), 0) >> 2
                pos = lax.broadcasted_iota(jnp.int32, (ROWS, D), 1)
                lo, hi = bounds(i, tok)
                halves = [
                    jnp.where((pos + c >= lo) & (pos + c < hi), s[:, c : c + D], NEG)
                    for c in range(0, TOK, D)
                ]
                s = jnp.concatenate(halves, axis=1)
            sscr[i] = s
            mscr[...] = jnp.maximum(mscr[...], jnp.maximum(s[:, 0:D], s[:, D : 2 * D]))

        def first_pass(i, _, state=state, scores=scores):
            st = state(i)
            pl.when(st == 1)(lambda: scores(True, i))
            pl.when(st == 2)(lambda: scores(False, i))
            return 0

        mscr[...] = before[3 * j + 1][...] if merge else jnp.full((ROWS, D), NEG, jnp.float32)
        lax.fori_loop(0, nb, first_pass, 0)
        m = jnp.max(mscr[...], axis=1, keepdims=True)
        if merge:
            shrink = jnp.exp2((before[3 * j + 1][...] - m) * SCALE2)
            acc[...] = before[3 * j][...] * shrink
            lscr[...] = before[3 * j + 2][...] * shrink
        else:
            acc[...] = jnp.zeros_like(acc)
            lscr[...] = jnp.zeros_like(lscr)
        mscr[...] = jnp.broadcast_to(m, (ROWS, D))

        def weigh(i):
            s = sscr[i]
            top = mscr[...]
            lo = jnp.exp2((s[:, 0:D] - top) * SCALE2)
            hi = jnp.exp2((s[:, D : 2 * D] - top) * SCALE2)
            lscr[...] += lo + hi
            p = jnp.concatenate([lo.astype(jnp.bfloat16), hi.astype(jnp.bfloat16)], axis=1)
            acc[...] += jnp.dot(p, vscr[i], preferred_element_type=jnp.float32)

        def second_pass(i, _, state=state):
            pl.when(state(i) > 0)(lambda: weigh(i))
            return 0

        lax.fori_loop(0, nb, second_pass, 0)
        if last == "state":
            outs[3 * j][...] = acc[...]
            outs[3 * j + 1][...] = mscr[...]
            outs[3 * j + 2][...] = lscr[...]
            continue
        total = jnp.maximum(jnp.sum(lscr[...], axis=1, keepdims=True), 1e-30)
        outs[per * j][0:ROWS, :] = (acc[...] * (1.0 / total)).astype(outs[per * j].dtype)
        lse = jnp.broadcast_to(m * SCALE + jnp.log(total), (ROWS, D))
        for g in range(GROUPS):
            rows_scr[g : g + 1, :] = lse[g * HALF : (g + 1) * HALF, :].T[0:1, :]
        if last == "keep":
            outs[2 * j + 1][...] = rows_scr[...]
        elif last == "send":
            rest = rows_scr[...]
            for t in range(3):
                part = rest.astype(jnp.bfloat16)
                outs[j][ROWS + t * GROUPS : ROWS + (t + 1) * GROUPS, :] = part
                rest = rest - part.astype(jnp.float32)


def attn(deltas, blocks, kv, qs, before, last):
    n, nb = len(deltas), len(blocks)
    args = (*kv, *qs, *before)
    wide = jax.ShapeDtypeStruct((ROWS, D), jnp.float32)
    outs = {
        "state": [wide] * 3,
        "send": [jax.ShapeDtypeStruct((ROWS + 3 * GROUPS, D), jnp.bfloat16)],
        "keep": [wide, jax.ShapeDtypeStruct((GROUPS, D), jnp.float32)],
    }[last] * n
    return pl.pallas_call(
        functools.partial(attn_kernel, deltas, blocks, bool(before), last),
        out_shape=outs,
        in_specs=[VM] * len(args),
        out_specs=[VM] * len(outs),
        scratch_shapes=[
            pltpu.VMEM((nb, TOK, D), jnp.bfloat16),
            pltpu.VMEM((nb, TOK, D), jnp.bfloat16),
            pltpu.VMEM((nb, ROWS, TOK), jnp.float32),
            pltpu.VMEM((ROWS, D), jnp.float32),
            pltpu.VMEM((ROWS, D), jnp.float32),
            pltpu.VMEM((ROWS, D), jnp.float32),
            pltpu.VMEM((GROUPS, D), jnp.float32),
            pltpu.SMEM((nb, 4), jnp.int32),
        ],
        compiler_params=pltpu.CompilerParams(vmem_limit_bytes=20 * MIB),
        cost_estimate=pl.CostEstimate(
            flops=4 * ROWS * D * TOK * nb * n,
            bytes_accessed=MIB,
            transcendentals=ROWS * TOK * nb * n,
        ),
    )(*args)


def combine_kernel(a_ref, lse_ref, b_ref, c_ref, o_ref, scr):
    x = lax.axis_index("x")

    def lse_of(ref, delta):
        terms = [
            ref[ROWS + t * GROUPS : ROWS + (t + 1) * GROUPS, :].astype(jnp.float32)
            for t in range(3)
        ]
        return jnp.where(x >= delta, terms[0] + (terms[1] + terms[2]), NEG)

    lses = (lse_ref[...], lse_of(b_ref, 1), lse_of(c_ref, 2))
    top = jnp.maximum(jnp.maximum(lses[0], lses[1]), lses[2])
    ws = [jnp.exp(lse - top) for lse in lses]
    inv = 1.0 / (ws[0] + ws[1] + ws[2])
    pad = jnp.zeros((HALF - GROUPS, D), jnp.float32)
    ws = [jnp.concatenate([w * inv, pad], axis=0).T for w in ws]
    for g in range(GROUPS):
        rows = slice(g * HALF, (g + 1) * HALF)
        scr[rows, :] = sum(
            ref[rows, :].astype(jnp.float32) * w[:, g : g + 1]
            for ref, w in zip((a_ref, b_ref, c_ref), ws)
        )
    for h in range(HEADS):
        rows = pl.ds(h, TOK, stride=HEADS)
        o_ref[:, h * D : (h + 1) * D] = scr[rows, :].astype(o_ref.dtype)


def combine(*args):
    return pl.pallas_call(
        combine_kernel,
        out_shape=jax.ShapeDtypeStruct((TOK, HEADS * D), jnp.bfloat16),
        in_specs=[VM] * len(args),
        out_specs=VM,
        scratch_shapes=[pltpu.VMEM((ROWS, D), jnp.float32)],
        compiler_params=pltpu.CompilerParams(vmem_limit_bytes=6 * MIB),
    )(*args)


def along(a, axis, shift, n):
    pairs = [(i, i + shift) for i in range(n)]
    if axis == "x":
        pairs = [(i, j) for i, j in pairs if 0 <= j < n]
    return lax.ppermute(a, axis, [(i, j % n) for i, j in pairs])


def local(queries, keys, values, doc_ids):
    kv, q = prep(
        keys.reshape(TOK, D), values.reshape(TOK, D), queries.reshape(ROWS, D), doc_ids.reshape(2, D)
    )
    up2 = along(kv, "z", 2, NZ)
    dn2 = along(kv, "z", -2, NZ)
    q2 = along(q, "x", -2, NX)
    q1 = along(q, "x", -1, NX)
    up13 = along(jnp.concatenate([kv, up2], axis=0), "z", 1, NZ)
    dn13 = along(jnp.concatenate([kv, dn2], axis=0), "z", -1, NZ)
    far_k = along(up2[0:TOK], "z", 2, NZ)
    far_v = along(dn2[TOK:PIECE], "z", -2, NZ)
    first, rest, end = [kv, up2, dn2], [up13, dn13], [far_k, far_v]
    near1 = attn((1,), NEAR, first, [q1], (), "state")
    near2 = attn((2,), NEAR, first, [q2], (), "state")
    mid = attn((2, 1), MID, rest, [q2, q1], (*near2, *near1), "state")
    mid2, mid1 = mid[:3], mid[3:]
    (o2,) = attn((2,), LAST, end, [q2], mid2, "send")
    r2 = along(o2, "x", 2, NX)
    (o1,) = attn((1,), LAST, end, [q1], mid1, "send")
    r1 = along(o1, "x", 1, NX)
    o0, lse0 = attn((0,), EVERY, first + rest + end, [q], (), "keep")
    merged = combine(o0, lse0, r1, r2)
    return lax.all_to_all(merged, ("y", "core"), split_axis=0, concat_axis=1, tiled=True)


def solution(mesh):
    grid = Mesh(mesh.devices.reshape(NX, NZ, 4, 2), ("x", "z", "y", "core"))
    ctx, head = ("x", "z"), ("y", "core")
    return jax.shard_map(
        local,
        mesh=grid,
        in_specs=(P(ctx, head, None), P(ctx, head, None), P(ctx, head, None), P(ctx)),
        out_specs=P(ctx + head, None),
        check_vma=False,
    )
```
